32 devices in a mesh: stn: 8 (over z, core), win: 4 (over y, x).
Axes of the slice: x: 2, y: 2, z: 4, core: 2. Of those that a mesh axis runs over, the one named last changes fastest.
Arguments:
- records: bfloat16 [128, 4, 3, 8192], P('stn', 'win'), may hold values from -6 to 6
- observed: float32 [128, 3, 3, 256], P('stn'), may hold values from -6 to 6
- lag_lo: int32 [128], P('stn'), may hold values from 0 to 63
- lag_hi: int32 [128], P('stn'), may hold values from 192 to 256
- send_table: int32 [8, 8, 1], P('stn'), may hold values from 0 to 15, as said below
- pair_first: int32 [128], P('stn'), may hold values from 0 to 7, as said below
- pair_second: int32 [128], P('stn'), may hold values from 0 to 7, as said below
Outputs:
- station_adjoint: bfloat16 [128, 4, 3, 8192], P('stn', 'win')
- residual: float32 [128, 3, 3, 256], P(('stn', 'win'))
The draws below stay inside these ranges and needn't reach their ends.
Inputs may be any that keep to these rules, and one draw needn't show every extreme that they name: Each entry send_table[g, o, :] names 1 different local stations of group g. `pair_first`: slot indices at the pair's owner; a pair's two slots differ, no two pairs of an owner join the same two slots, and every slot of an owner is named by some pair. `pair_second`: slot indices at the pair's owner, as for pair_first.
All inputs are finite; a program needn't handle non-finite values.
Results may differ from the reference program's by a relative error of at most 0.0053.
Values may be sent and summed in bfloat16 or wider, within the bound.
No kernel may reach another device: no remote copies, remote signals or barrier semaphores. Data moves between devices by JAX's collectives and lax.ppermute only.
A program may use at most 192 MiB of HBM per device.

```python
import math
import jax
import jax.numpy as jnp
from jax import lax

STAT_DEV = 16
OWNERS = 8
STATIONS = 128
WINDOWS = 4
SAMPLES = 8192
LAGS = 256
CAP = 1
SLOTS = 8
PAIR_DEV = 16
PAIRS = 128


def draw_send_table(key, part):
    subkeys = jax.random.split(jax.random.fold_in(key, 11), OWNERS * OWNERS)
    chosen = jax.vmap(lambda subkey: jax.random.permutation(subkey, STAT_DEV))(subkeys)[:, :CAP]
    return chosen.reshape(OWNERS, OWNERS, CAP).astype(jnp.int32)


def pair_slots(key):
    subkeys = jax.random.split(jax.random.fold_in(key, 7), OWNERS)
    orders = jax.vmap(lambda subkey: jax.random.permutation(subkey, SLOTS))(subkeys)
    offsets = jnp.arange(PAIR_DEV, dtype=jnp.int32)
    shifts = 1 + offsets // SLOTS
    firsts = orders[:, offsets % SLOTS]
    seconds = orders[:, (offsets + shifts) % SLOTS]
    return (firsts.reshape(PAIRS).astype(jnp.int32), seconds.reshape(PAIRS).astype(jnp.int32))


def draw_pair_first(key, part):
    return pair_slots(key)[0]


def draw_pair_second(key, part):
    return pair_slots(key)[1]


def plant(values, rng, low, high):
    longest = values.shape.index(max(values.shape))
    spots = []
    for shift in (0, 1):
        where = [jax.random.randint(jax.random.fold_in(rng, axis), (), 0, length) for axis, length in enumerate(values.shape)]
        where[longest] = (where[longest] + shift) % values.shape[longest]
        spots.append(tuple(where))
    return values.at[spots[0]].set(low).at[spots[1]].set(high)


def block_levels(key, extent, pieces, low, largest):
    loudness, own = 1.0, jax.random.fold_in(key, 6)
    for dim, shards_of in pieces:
        draws = jnp.exp(jax.random.uniform(jax.random.fold_in(own, dim), (shards_of,), jnp.float32, low / len(pieces), largest / len(pieces)))
        loudness = loudness * jnp.repeat(draws, extent[dim] // shards_of).reshape([-1 if axis == dim else 1 for axis in range(len(extent))])
    return loudness


def centred(stream_key, extent, width, bound, shards=(), kind=jnp.bfloat16):
    level = block_levels(stream_key, extent, shards, -0.22, 0.18) if shards else 1.0
    result = jax.random.normal(stream_key, extent, jnp.float32) * width * level
    return jnp.minimum(jnp.maximum(result, -bound), bound).astype(kind)


def setup_inputs(seed: int = 0) -> dict:
    key_of = jax.random.split(jax.random.key(seed), 8)
    records = centred(key_of[0], (STATIONS, WINDOWS, 3, SAMPLES), 1.0, 6.0, ((0, 8), (1, 4)))
    observed = centred(key_of[1], (PAIRS, 3, 3, LAGS), 1.0, 6.0, ((0, 8),), jnp.float32)
    lag_lo = plant(jax.random.randint(key_of[2], (PAIRS,), 0, LAGS // 4), jax.random.fold_in(key_of[2], 1), 0, (LAGS // 4) - 1).astype(jnp.int32)
    lag_hi = plant(jax.random.randint(key_of[3], (PAIRS,), 3 * LAGS // 4, LAGS + 1), jax.random.fold_in(key_of[3], 1), 3 * LAGS // 4, LAGS).astype(jnp.int32)
    send_table = draw_send_table(jax.random.fold_in(key_of[7], 71), 0)
    pair_first = draw_pair_first(jax.random.fold_in(key_of[7], 71), 0)
    pair_second = draw_pair_second(jax.random.fold_in(key_of[7], 71), 0)
    return dict(records=records, observed=observed, lag_lo=lag_lo, lag_hi=lag_hi, send_table=send_table, pair_first=pair_first, pair_second=pair_second)


def lag_panels(series):
    lag_count = LAGS
    half_lag = lag_count // 2
    leading = series.shape[:-1]
    padded = jnp.pad(series, [(0, 0)] * len(leading) + [(half_lag, lag_count - half_lag)])
    blocks = padded.reshape(leading + (series.shape[-1] // lag_count + 1, lag_count))
    return jnp.concatenate([blocks[..., :-1, :], blocks[..., 1:, :]], axis=-1)

def panel_adjoint(grads):
    lag_count = LAGS
    half_lag = lag_count // 2
    leading = grads.shape[:-2]
    block_total = grads.shape[-2]
    spacer = [(0, 0)] * len(leading)
    low_part = jnp.pad(grads[..., :lag_count], spacer + [(0, 1), (0, 0)])
    high_part = jnp.pad(grads[..., lag_count:], spacer + [(1, 0), (0, 0)])
    joined = (low_part + high_part).reshape(leading + ((block_total + 1) * lag_count,))
    return joined[..., half_lag:half_lag + block_total * lag_count]

def diagonal_sums(products):
    leading = products.shape[:-2]
    rows_count = products.shape[-2]
    flattened = products.reshape(leading + (2 * rows_count * rows_count,))
    flattened = jnp.concatenate([flattened, jnp.zeros(leading + (rows_count,), products.dtype)], axis=-1)
    return lax.optimization_barrier(jnp.sum(flattened.reshape(leading + (rows_count, 2 * rows_count + 1))[..., :rows_count], axis=-2))

def lag_toeplitz(source):
    leading = source.shape[:-1]
    lag_count = source.shape[-1]
    padded_row = jnp.concatenate([source, jnp.zeros(leading + (lag_count + 1,), source.dtype)], axis=-1)
    repeated = jnp.broadcast_to(padded_row[..., None, :], leading + (lag_count, 2 * lag_count + 1))
    repeated = repeated.reshape(leading + (lag_count * (2 * lag_count + 1),))
    return repeated[..., :2 * lag_count * lag_count].reshape(leading + (lag_count, 2 * lag_count))

def reference(records, observed, lag_lo, lag_hi, send_table, pair_first, pair_second):
    source_ids = jnp.arange(OWNERS, dtype=jnp.int32)
    stations_of = source_ids[:, None, None] * STAT_DEV + send_table
    slot_stations = jnp.transpose(stations_of, (1, 0, 2)).reshape(OWNERS, SLOTS).astype(jnp.int32)
    firsts_all = pair_first.reshape(OWNERS, PAIR_DEV)
    seconds_all = pair_second.reshape(OWNERS, PAIR_DEV)
    lag_index = jnp.arange(LAGS, dtype=jnp.int32)
    lag_mask = (lag_index[None, :] >= lag_lo[:, None]) & (lag_index[None, :] < lag_hi[:, None])
    lag_mask = lag_mask.reshape(OWNERS, PAIR_DEV, LAGS)
    observed_all = observed.reshape(OWNERS, PAIR_DEV, 3, 3, LAGS)
    corr_scale = 1.0 / math.sqrt(SAMPLES * WINDOWS)
    adj_scale = 1.0 / math.sqrt(3 * LAGS)
    highest = lax.Precision.HIGHEST

    def owner_step(accumulated, inputs):
        stations, firsts, seconds, observed_own, mask_own = inputs
        slot_records = jnp.take(records, stations, axis=0).astype(jnp.float32)
        first_part = jnp.take(slot_records, firsts, axis=0).reshape(PAIR_DEV, WINDOWS, 3, SAMPLES // LAGS, LAGS)
        second_part = lag_panels(jnp.take(slot_records, seconds, axis=0))
        products = jnp.einsum('pwaks,pwbku->pabsu', first_part, second_part, precision=highest)
        stacked = diagonal_sums(products) * corr_scale
        residual = jnp.where(mask_own[:, None, None, :], stacked - observed_own, jnp.float32(0.0))
        rounded = lax.optimization_barrier(residual.astype(jnp.bfloat16))
        kernel = lag_toeplitz(rounded.astype(jnp.float32))
        first_grad = jnp.einsum('pabsu,pwbku->pwaks', kernel, second_part, precision=highest)
        second_grad = panel_adjoint(jnp.einsum('pabsu,pwaks->pwbku', kernel, first_part, precision=highest))
        first_grad = first_grad.reshape(PAIR_DEV, WINDOWS * 3 * SAMPLES)
        second_grad = second_grad.reshape(PAIR_DEV, WINDOWS * 3 * SAMPLES)
        slot_sum = jax.ops.segment_sum(first_grad, firsts, num_segments=SLOTS)
        slot_sum = slot_sum + jax.ops.segment_sum(second_grad, seconds, num_segments=SLOTS)
        slot_adjoint = (slot_sum * adj_scale).astype(jnp.bfloat16)
        accumulated = accumulated.at[stations].add(slot_adjoint.astype(jnp.float32).reshape(SLOTS, WINDOWS, 3, SAMPLES))
        return (accumulated, residual)
    initial = jnp.zeros((STATIONS, WINDOWS, 3, SAMPLES), jnp.float32)
    summed, residuals = lax.scan(owner_step, initial, (slot_stations, firsts_all, seconds_all, observed_all, lag_mask))
    return (summed.astype(jnp.bfloat16), residuals.reshape(PAIRS, 3, 3, LAGS))
```

```python
import functools
import math

import jax
import jax.numpy as jnp
from jax import lax
from jax.experimental import pallas as pl
from jax.experimental.pallas import tpu as pltpu
from jax.sharding import PartitionSpec as P

LAGS = 256
HALF = LAGS // 2
LANES = 128
PHASES = 16
SPAN = LAGS + PHASES
CHANS = 3
WINDOW = 3 * LANES
DEPTH = 7 * LANES
TAIL = DEPTH - CHANS * SPAN


def pack_kernel(rows_ref, rec_ref, out_ref, scratch):
    stations = rec_ref.shape[1]
    chunks = rec_ref.shape[2] // LANES
    for r in range(chunks):
        piece = rec_ref[0, :, r * LANES:(r + 1) * LANES]
        scratch[r * stations:(r + 1) * stations, :] = piece.astype(jnp.float32)
    for d in range(out_ref.shape[0]):
        picked = scratch[pl.ds(rows_ref[d], chunks, stride=stations), :]
        out_ref[d, 0] = picked.astype(jnp.bfloat16)


def unpack_kernel(rows_ref, ret_ref, out_ref, scratch):
    stations = out_ref.shape[1]
    chunks = out_ref.shape[2] // LANES
    scratch[...] = jnp.zeros_like(scratch)
    for d in range(ret_ref.shape[0]):
        where = pl.ds(rows_ref[d], chunks, stride=stations)
        scratch[where, :] = scratch[where, :] + ret_ref[d, 0].astype(jnp.float32)
    for r in range(chunks):
        piece = scratch[r * stations:(r + 1) * stations, :]
        out_ref[0, :, r * LANES:(r + 1) * LANES] = piece.astype(jnp.bfloat16)


def build_phases(slot_ref, fan_ref):
    chunks = slot_ref.shape[1]
    rows = fan_ref.shape[1]
    lane = lax.broadcasted_iota(jnp.int32, (LANES, LANES), 1)
    full_lane = lax.broadcasted_iota(jnp.int32, (rows, LANES), 1)

    def step(g, carry):
        pair = slot_ref[pl.ds(2 * g, 2)].astype(jnp.float32).reshape(2 * chunks, LANES)
        middle = pair.T
        before = jnp.where(lane % chunks == 0, 0.0, pltpu.roll(middle, 1, 1))
        after = jnp.where(lane % chunks == chunks - 1, 0.0, pltpu.roll(middle, LANES - 1, 1))
        wide = jnp.concatenate([before, middle, after], axis=0)
        swapped = pltpu.roll(wide, chunks, 1)
        left = full_lane < chunks
        fan_ref[2 * g] = jnp.where(left, wide[:rows], swapped[PHASES:]).astype(jnp.bfloat16)
        fan_ref[2 * g + 1] = jnp.where(left, swapped[:rows], wide[PHASES:]).astype(jnp.bfloat16)
        return carry

    lax.fori_loop(0, slot_ref.shape[0] // 2, step, 0)


def shifted_rows(fan_ref, slot):
    columns = []
    for m in range(4):
        first = 2 * PHASES * m
        parts = [fan_ref[CHANS * slot + b, first:first + SPAN, :] for b in range(CHANS)]
        parts.append(fan_ref[CHANS * slot, first:first + TAIL, :])
        columns.append(jnp.concatenate(parts, axis=0))
    return jnp.concatenate(columns, axis=1)


def corr_kernel(first_ref, second_ref, slot_ref, corr_ref, fan_ref, heads):
    build_phases(slot_ref, fan_ref)
    height = CHANS * PHASES
    row = lax.broadcasted_iota(jnp.int32, (height, height), 0)
    column = lax.broadcasted_iota(jnp.int32, (height, height), 1)
    same = row // PHASES == column // PHASES
    flip = (same & (row % PHASES + column % PHASES == PHASES - 1)).astype(jnp.bfloat16)

    def head(q, carry):
        rows = []
        for a in range(CHANS):
            pieces = []
            for m in range(4):
                start = HALF + 2 * PHASES * m
                pieces.append(fan_ref[CHANS * q + a, start:start + PHASES, :])
            rows.append(jnp.concatenate(pieces, axis=1))
        natural = jnp.concatenate(rows, axis=0)
        heads[q] = jnp.dot(flip, natural, preferred_element_type=jnp.float32).astype(jnp.bfloat16)
        return carry

    lax.fori_loop(0, heads.shape[0], head, 0)

    def step(p, carry):
        right = shifted_rows(fan_ref, second_ref[p])
        products = lax.dot_general(
            heads[first_ref[p]], right, (((1,), (1,)), ((), ())),
            preferred_element_type=jnp.float32,
        )
        for a in range(CHANS):
            for b in range(CHANS):
                block = products[PHASES * a:PHASES * (a + 1), LAGS * b:LAGS * b + WINDOW]
                shift = WINDOW - PHASES * b - (PHASES - 1)
                turned = pltpu.roll(block, shift, 1, stride=1, stride_axis=0)
                corr_ref[CHANS * a + b, pl.ds(p, 1), :] = jnp.sum(
                    turned[:, :LAGS], axis=0, keepdims=True
                )
        return carry

    lax.fori_loop(0, corr_ref.shape[1], step, 0)


def spread(lag_rows, base, stride_rows):
    turned = []
    for c in range(CHANS):
        row = lag_rows[pl.ds(base + stride_rows * c, 1), :]
        block = jnp.broadcast_to(row, (PHASES, WINDOW))
        turned.append(pltpu.roll(block, PHASES * c, 1, stride=1, stride_axis=0))
    w0, w1, w2 = turned
    return jnp.concatenate(
        [
            w0[:, :LAGS],
            w0[:, LAGS:] + w1[:, :LANES],
            w1[:, LANES:LAGS],
            w1[:, LAGS:] + w2[:, :LANES],
            w2[:, LANES:],
        ],
        axis=1,
    ).astype(jnp.bfloat16)


def adjoint_kernel(
    corr_scale, adj_scale, first_ref, second_ref, offset_ref,
    parts_ref, observed_ref, low_ref, high_ref, fan_ref,
    out_ref, share_ref, resid, forward, backward, bands, total,
):
    pairs = observed_ref.shape[1]
    combos = observed_ref.shape[0]
    slots = bands.shape[0]
    lag = lax.broadcasted_iota(jnp.int32, (pairs, LAGS), 1)
    inside = (lag >= low_ref[...]) & (lag < high_ref[...])
    flip = (
        lax.broadcasted_iota(jnp.int32, (LAGS, WINDOW), 0)
        + lax.broadcasted_iota(jnp.int32, (LAGS, WINDOW), 1)
        == LAGS
    ).astype(jnp.bfloat16)
    forward[...] = jnp.zeros_like(forward)
    for i in range(combos):
        summed = parts_ref[0, i]
        for w in range(1, parts_ref.shape[0]):
            summed = summed + parts_ref[w, i]
        value = jnp.where(inside, summed * corr_scale - observed_ref[i], 0.0)
        resid[i] = value
        rounded = value.astype(jnp.bfloat16)
        forward[i * pairs:(i + 1) * pairs, :LAGS] = rounded.astype(jnp.float32)
        backward[i * pairs:(i + 1) * pairs, :] = jnp.dot(
            rounded, flip, preferred_element_type=jnp.float32
        )
        for j in range(share_ref.shape[1]):
            share_ref[i, j:j + 1, :] = resid[i, pl.ds(offset_ref[0] + j, 1), :]

    bands[...] = jnp.zeros_like(bands)
    height = CHANS * PHASES

    def fill(p, carry):
        qf = first_ref[p]
        qs = second_ref[p]
        for c in range(CHANS):
            start = pl.multiple_of(height * qf + PHASES * c, PHASES)
            bands[qs, pl.ds(start, PHASES), :] = spread(forward, CHANS * pairs * c + p, pairs)
            start = pl.multiple_of(height * qs + PHASES * c, PHASES)
            bands[qf, pl.ds(start, PHASES), :] = spread(backward, pairs * c + p, CHANS * pairs)
        return carry

    lax.fori_loop(0, pairs, fill, 0)
    total[...] = jnp.zeros_like(total)

    def accumulate(r, carry):
        right = shifted_rows(fan_ref, r)
        total[...] += jnp.dot(bands[r], right, preferred_element_type=jnp.float32)
        return carry

    lax.fori_loop(0, slots, accumulate, 0)
    chunks = out_ref.shape[1]
    left = lax.broadcasted_iota(jnp.int32, (PHASES, LANES), 1) < chunks

    def store(g, carry):
        base = pl.multiple_of(2 * PHASES * g, 2 * PHASES)
        pieces = []
        for m in range(4):
            one = total[pl.ds(base, PHASES), m * LANES:(m + 1) * LANES]
            two = total[pl.ds(base + PHASES, PHASES), m * LANES:(m + 1) * LANES]
            pieces.append(jnp.where(left, one, pltpu.roll(two, chunks, 1)))
            pieces.append(jnp.where(left, pltpu.roll(one, chunks, 1), two))
        tile = jnp.concatenate(pieces, axis=0).T * adj_scale
        out_ref[pl.ds(2 * g, 2)] = tile.reshape(2, chunks, LANES).astype(jnp.bfloat16)
        return carry

    lax.fori_loop(0, out_ref.shape[0] // 2, store, 0)


def smem():
    return pl.BlockSpec(memory_space=pltpu.SMEM)


def vmem():
    return pl.BlockSpec(memory_space=pltpu.VMEM)


def shards(records, observed, lag_lo, lag_hi, send_table, pair_first, pair_second):
    owner_count = lax.axis_size("stn")
    window_groups = lax.axis_size("win")
    stations, local_windows, _, samples = records.shape
    send_rows = send_table.reshape(-1)
    slots = send_rows.shape[0]
    chunks = samples // LANES
    pairs = observed.shape[0]
    combos = CHANS * CHANS
    share = pairs // window_groups
    corr_scale = 1.0 / math.sqrt(samples * local_windows * window_groups)
    adj_scale = 1.0 / math.sqrt(CHANS * LAGS)

    planes = jnp.transpose(records, (1, 2, 0, 3)).reshape(CHANS, stations, samples)
    outgoing = pl.pallas_call(
        pack_kernel,
        grid_spec=pltpu.PrefetchScalarGridSpec(
            num_scalar_prefetch=1,
            grid=(CHANS,),
            in_specs=[pl.BlockSpec((1, stations, samples), lambda c, rows: (c, 0, 0))],
            out_specs=pl.BlockSpec((slots, 1, chunks, LANES), lambda c, rows: (0, c, 0, 0)),
            scratch_shapes=[pltpu.VMEM((chunks * stations, LANES), jnp.float32)],
        ),
        out_shape=jax.ShapeDtypeStruct((slots, CHANS, chunks, LANES), jnp.bfloat16),
        name="pack",
    )(send_rows, planes)
    arrived = lax.all_to_all(outgoing, "stn", split_axis=0, concat_axis=0, tiled=True)

    rows = 3 * LANES - PHASES
    corr, fan = pl.pallas_call(
        corr_kernel,
        in_specs=[smem(), smem(), vmem()],
        out_specs=[vmem(), vmem()],
        out_shape=[
            jax.ShapeDtypeStruct((combos, pairs, LAGS), jnp.float32),
            jax.ShapeDtypeStruct((slots * CHANS, rows, LANES), jnp.bfloat16),
        ],
        scratch_shapes=[pltpu.VMEM((slots, CHANS * PHASES, 4 * LANES), jnp.bfloat16)],
        name="corr",
    )(pair_first, pair_second, arrived.reshape(slots * CHANS, chunks, LANES))
    parts = lax.all_gather(corr, "win")

    seen = jnp.transpose(observed, (1, 2, 0, 3)).reshape(combos, pairs, LAGS)
    offset = (lax.axis_index("win") * share).astype(jnp.int32).reshape(1)
    slot_adjoint, residual = pl.pallas_call(
        functools.partial(adjoint_kernel, corr_scale, adj_scale),
        in_specs=[smem(), smem(), smem(), vmem(), vmem(), vmem(), vmem(), vmem()],
        out_specs=[vmem(), vmem()],
        out_shape=[
            jax.ShapeDtypeStruct((slots * CHANS, chunks, LANES), jnp.bfloat16),
            jax.ShapeDtypeStruct((combos, share, LAGS), jnp.float32),
        ],
        scratch_shapes=[
            pltpu.VMEM((combos, pairs, LAGS), jnp.float32),
            pltpu.VMEM((combos * pairs, WINDOW), jnp.float32),
            pltpu.VMEM((combos * pairs, WINDOW), jnp.float32),
            pltpu.VMEM((slots, slots * CHANS * PHASES, DEPTH), jnp.bfloat16),
            pltpu.VMEM((slots * CHANS * PHASES, 4 * LANES), jnp.float32),
        ],
        compiler_params=pltpu.CompilerParams(vmem_limit_bytes=44 * 2**20),
        name="adjoint",
    )(
        pair_first, pair_second, offset, parts, seen,
        lag_lo.reshape(pairs, 1), lag_hi.reshape(pairs, 1), fan,
    )
    returned = lax.all_to_all(
        slot_adjoint.reshape(slots, CHANS, chunks, LANES),
        "stn", split_axis=0, concat_axis=0, tiled=True,
    )
    stacked = pl.pallas_call(
        unpack_kernel,
        grid_spec=pltpu.PrefetchScalarGridSpec(
            num_scalar_prefetch=1,
            grid=(CHANS,),
            in_specs=[pl.BlockSpec((slots, 1, chunks, LANES), lambda c, rows: (0, c, 0, 0))],
            out_specs=pl.BlockSpec((1, stations, samples), lambda c, rows: (c, 0, 0)),
            scratch_shapes=[pltpu.VMEM((chunks * stations, LANES), jnp.float32)],
        ),
        out_shape=jax.ShapeDtypeStruct((CHANS, stations, samples), jnp.bfloat16),
        name="unpack",
    )(send_rows, returned)
    station_adjoint = jnp.transpose(stacked.reshape(1, CHANS, stations, samples), (2, 0, 1, 3))
    residual = jnp.transpose(residual.reshape(CHANS, CHANS, share, LAGS), (2, 0, 1, 3))
    return (station_adjoint, residual)


def solution(mesh):
    placed = (
        P("stn", "win", None, None),
        P("stn", None, None, None),
        P("stn"),
        P("stn"),
        P("stn", None, None),
        P("stn"),
        P("stn"),
    )
    return jax.shard_map(
        shards,
        mesh=mesh,
        in_specs=placed,
        out_specs=(P("stn", "win", None, None), P(("stn", "win"), None, None, None)),
        check_vma=False,
    )
```

```python
import functools
import math

import jax
import jax.numpy as jnp
from jax import lax
from jax.experimental import pallas as pl
from jax.experimental.pallas import tpu as pltpu
from jax.sharding import PartitionSpec as P

LAGS = 256
HALF = LAGS // 2
LANES = 128
HALF_TILE = LANES // 2
PHASES = 16
WIDE = 32
CHANS = 3
WINDOW = 3 * LANES
DEPTH = 7 * LANES


def pack_kernel(rows_ref, rec_ref, swap_ref, *refs):
    keep_refs = refs[:-3]
    buffer, scratch, sems = refs[-3:]
    me = lax.axis_index("stn")
    stations = rec_ref.shape[1]
    chunks = rec_ref.shape[2] // LANES
    copies = [
        pltpu.make_async_copy(rec_ref.at[c], buffer.at[c], sems.at[c]) for c in range(CHANS)
    ]
    for copy in copies:
        copy.start()
    for c in range(CHANS):
        copies[c].wait()
        for r in range(chunks):
            piece = buffer[c, :, r * LANES:(r + 1) * LANES]
            scratch[c, r * stations:(r + 1) * stations, :] = piece.astype(jnp.float32)
        for j, keep_ref in enumerate(keep_refs):
            for i, ref in enumerate((keep_ref, swap_ref.at[j])):
                station = rows_ref[me ^ (2 * j + i)]
                picked = scratch[c, pl.ds(station, chunks, stride=stations), :]
                ref[c] = picked.astype(jnp.bfloat16)


def unpack_kernel(order, rows_ref, *refs):
    returned = refs[:-4]
    out_ref, buffer, scratch, sems = refs[-4:]
    me = lax.axis_index("stn")
    stations = out_ref.shape[1]
    chunks = out_ref.shape[2] // LANES
    copies = []
    for c in range(CHANS):
        scratch[c] = jnp.zeros_like(scratch[c])
        pieces = [(2 * j + i, ref.at[i]) for j, ref in zip(order, returned[:-2]) for i in range(2)]
        for j, ref in pieces + [(0, returned[-2]), (1, returned[-1])]:
            where = pl.ds(rows_ref[me ^ j], chunks, stride=stations)
            scratch[c, where, :] = scratch[c, where, :] + ref[c].astype(jnp.float32)
        for r in range(chunks):
            piece = scratch[c, r * stations:(r + 1) * stations, :]
            buffer[c, :, r * LANES:(r + 1) * LANES] = piece.astype(jnp.bfloat16)
        copies.append(pltpu.make_async_copy(buffer.at[c], out_ref.at[c], sems.at[c]))
        copies[c].start()
    for copy in copies:
        copy.wait()


def build_phases(slot_refs, fan_ref):
    chunks = slot_refs[0].shape[1]
    rows = fan_ref.shape[1]
    lane = lax.broadcasted_iota(jnp.int32, (LANES, LANES), 1)
    left = lax.broadcasted_iota(jnp.int32, (rows, LANES), 1) < chunks
    for place in range(0, CHANS * len(slot_refs), 2):
        pair = [slot_refs[e // CHANS][e % CHANS] for e in (place, place + 1)]
        middle = jnp.concatenate(pair, axis=0).astype(jnp.float32).T
        before = jnp.where(lane % chunks == 0, 0.0, pltpu.roll(middle, 1, 1))
        after = jnp.where(lane % chunks == chunks - 1, 0.0, pltpu.roll(middle, LANES - 1, 1))
        wide = jnp.concatenate([before, middle, after], axis=0)
        swapped = pltpu.roll(wide, chunks, 1)
        one = jnp.where(left, wide[:rows], swapped[HALF_TILE:])
        two = jnp.where(left, swapped[:rows], wide[HALF_TILE:])
        fan_ref[place] = one.astype(jnp.bfloat16)
        fan_ref[place + 1] = two.astype(jnp.bfloat16)


def shifted_rows(fan_ref, slot, phases):
    span = LAGS + phases
    tail = DEPTH - CHANS * span
    columns = []
    for first in range(0, HALF_TILE, phases):
        parts = [fan_ref[CHANS * slot + b, first:first + span, :] for b in range(CHANS)]
        parts.append(fan_ref[CHANS * slot, first:first + tail, :])
        columns.append(jnp.concatenate(parts, axis=0))
    return jnp.concatenate(columns, axis=1)


def fetch(sources, targets, sems):
    copies = [pltpu.make_async_copy(s, t, sems.at[k]) for k, (s, t) in enumerate(zip(sources, targets))]
    for copy in copies:
        copy.start()
    return copies


def corr_kernel(order, first_in, second_in, *refs):
    given = refs[:-6]
    corr_ref, fan_ref, heads, first_ref, second_ref, sems = refs[-6:]
    copies = fetch((first_in, second_in), (first_ref, second_ref), sems)
    me = lax.axis_index("stn")
    slot_refs = [None] * (2 * len(given) - 2)
    for j, ref in zip(order, given[:-2]):
        slot_refs[2 * j:2 * j + 2] = [ref.at[0], ref.at[1]]
    slot_refs[:2] = given[-2:]
    build_phases(slot_refs, fan_ref)
    height = CHANS * WIDE
    row = lax.broadcasted_iota(jnp.int32, (height, height), 0)
    column = lax.broadcasted_iota(jnp.int32, (height, height), 1)
    same = row // WIDE == column // WIDE
    flip = (same & (row % WIDE + column % WIDE == WIDE - 1)).astype(jnp.bfloat16)

    def head(q, carry):
        rows = []
        for a in range(CHANS):
            pieces = []
            for m in range(0, HALF_TILE, WIDE):
                pieces.append(fan_ref[CHANS * q + a, HALF + m:HALF + m + WIDE, :])
            rows.append(jnp.concatenate(pieces, axis=1))
        natural = jnp.concatenate(rows, axis=0)
        heads[q] = jnp.dot(flip, natural, preferred_element_type=jnp.float32).astype(jnp.bfloat16)
        return carry

    lax.fori_loop(0, heads.shape[0], head, 0, unroll=8)
    for copy in copies:
        copy.wait()

    def step(p, carry):
        right = shifted_rows(fan_ref, second_ref[p] ^ me, WIDE)
        products = lax.dot_general(
            heads[first_ref[p] ^ me], right, (((1,), (1,)), ((), ())),
            preferred_element_type=jnp.float32,
        )
        for a in range(CHANS):
            for b in range(CHANS):
                block = products[WIDE * a:WIDE * (a + 1), LAGS * b:LAGS * b + WINDOW]
                shift = WINDOW - WIDE * b - (WIDE - 1)
                turned = pltpu.roll(block, shift, 1, stride=1, stride_axis=0)
                corr_ref[CHANS * a + b, pl.ds(p, 1), :] = jnp.sum(
                    turned[:, :LAGS], axis=0, keepdims=True
                )
        return carry

    lax.fori_loop(0, corr_ref.shape[1], step, 0, unroll=8)


def spread(lag_rows, base, stride_rows):
    turned = []
    for c in range(CHANS):
        row = lag_rows[pl.ds(base + stride_rows * c, 1), :]
        block = jnp.broadcast_to(row, (PHASES, WINDOW))
        turned.append(pltpu.roll(block, PHASES * c, 1, stride=1, stride_axis=0))
    w0, w1, w2 = turned
    return jnp.concatenate(
        [
            w0[:, :LAGS],
            w0[:, LAGS:] + w1[:, :LANES],
            w1[:, LANES:LAGS],
            w1[:, LAGS:] + w2[:, :LANES],
            w2[:, LANES:],
        ],
        axis=1,
    ).astype(jnp.bfloat16)


def pairwise(terms):
    while len(terms) > 1:
        terms = [sum(terms[k + 1:k + 2], terms[k]) for k in range(0, len(terms), 2)]
    return terms[0]


def adjoint_kernel(
    corr_scale, adj_scale, first_in, second_in, low_in, high_in, observed_ref, fan_ref, *refs
):
    first_ref, second_ref, low_ref, high_ref, sems = refs[-5:]
    refs = refs[:-5]
    copies = fetch(
        (first_in, second_in, low_in, high_in), (first_ref, second_ref, low_ref, high_ref), sems
    )
    me = lax.axis_index("stn")
    chips = fan_ref.shape[0] // (2 * CHANS)
    part_refs = refs[:-chips - 7]
    keep_refs = refs[-chips - 7:-7]
    swap_ref, share_ref, resid, forward, backward, bands, total = refs[-7:]
    pairs = observed_ref.shape[1]
    combos = observed_ref.shape[0]
    slots = bands.shape[0]
    lag = lax.broadcasted_iota(jnp.int32, (pairs, LAGS), 1)
    bands[...] = jnp.zeros_like(bands)
    for copy in copies:
        copy.wait()
    row = lax.broadcasted_iota(jnp.int32, (pairs, LAGS), 0)
    low = jnp.zeros_like(row)
    high = jnp.zeros_like(row)
    for p in range(pairs):
        low = jnp.where(row == p, low_ref[p], low)
        high = jnp.where(row == p, high_ref[p], high)
    inside = (lag >= low) & (lag < high)
    offset = lax.axis_index("win") * share_ref.shape[1]
    flip = (
        lax.broadcasted_iota(jnp.int32, (LAGS, WINDOW), 0)
        + lax.broadcasted_iota(jnp.int32, (LAGS, WINDOW), 1)
        == LAGS
    ).astype(jnp.bfloat16)
    forward[...] = jnp.zeros_like(forward)
    for i in range(combos):
        summed = pairwise([ref[i] for ref in part_refs])
        value = jnp.where(inside, summed * corr_scale - observed_ref[i], 0.0)
        resid[i] = value
        rounded = value.astype(jnp.bfloat16)
        forward[i * pairs:(i + 1) * pairs, :LAGS] = rounded.astype(jnp.float32)
        backward[i * pairs:(i + 1) * pairs, :] = jnp.dot(
            rounded, flip, preferred_element_type=jnp.float32
        )
        for j in range(share_ref.shape[1]):
            share_ref[i, j:j + 1, :] = resid[i, pl.ds(offset + j, 1), :]

    height = CHANS * PHASES

    def row_place(q):
        return q // 2 + (slots // 2) * (1 - q % 2)

    def fill(p, carry):
        qf = first_ref[p] ^ me
        qs = second_ref[p] ^ me
        for c in range(CHANS):
            start = pl.multiple_of(height * row_place(qf) + PHASES * c, PHASES)
            bands[qs, pl.ds(start, PHASES), :] = spread(forward, CHANS * pairs * c + p, pairs)
            start = pl.multiple_of(height * row_place(qs) + PHASES * c, PHASES)
            bands[qf, pl.ds(start, PHASES), :] = spread(backward, pairs * c + p, CHANS * pairs)
        return carry

    lax.fori_loop(0, pairs, fill, 0, unroll=8)
    total[...] = jnp.zeros_like(total)

    def accumulate(r, carry):
        right = shifted_rows(fan_ref, r, PHASES)
        total[...] += jnp.dot(bands[r], right, preferred_element_type=jnp.float32)
        return carry

    lax.fori_loop(0, slots, accumulate, 0, unroll=8)
    chunks = swap_ref.shape[2]
    left = lax.broadcasted_iota(jnp.int32, (PHASES, LANES), 1) < chunks
    outs = [swap_ref.at[j] for j in range(chips)] + list(keep_refs)
    for place in range(0, CHANS * slots, 2):
        upper = []
        lower = []
        for m in range(4):
            columns = slice(m * LANES, (m + 1) * LANES)
            one = total[place * PHASES:(place + 1) * PHASES, columns]
            two = total[(place + 1) * PHASES:(place + 2) * PHASES, columns]
            upper.append(jnp.where(left, one, pltpu.roll(two, chunks, 1)))
            lower.append(jnp.where(left, pltpu.roll(one, chunks, 1), two))
        tile = (jnp.concatenate(upper + lower, axis=0).T * adj_scale).astype(jnp.bfloat16)
        for k in range(2):
            e = place + k
            outs[e // CHANS][e % CHANS] = tile[k * chunks:(k + 1) * chunks]


def smem():
    return pl.BlockSpec(memory_space=pltpu.SMEM)


def vmem():
    return pl.BlockSpec(memory_space=pltpu.VMEM)


def flipped(x, axis, bits):
    count = lax.axis_size(axis)
    return lax.ppermute(x, axis, [(k, k ^ bits) for k in range(count)])


def across(swap, keep):
    chips = len(keep)
    got = flipped(swap, "stn", 1)
    order = []
    blocks = []
    for j in range(chips - 1, 0, -1):
        moved = flipped(jnp.stack([keep[j], got[j]]), "stn", 2 * j)
        order.append(j)
        blocks.append(moved)
    return order + [0, 0], blocks + [keep[0], got[0]]


def window_parts(corr):
    groups = lax.axis_size("win")
    if groups > 4:
        gathered = lax.all_gather(corr, "win")
        return [gathered[w] for w in range(groups)]
    return [corr] + [flipped(corr, "win", w) for w in range(1, groups)]


def shards(records, observed, lag_lo, lag_hi, send_table, pair_first, pair_second):
    owner_count = lax.axis_size("stn")
    window_groups = lax.axis_size("win")
    stations, local_windows, _, samples = records.shape
    send_rows = send_table.reshape(-1)
    slots = send_rows.shape[0]
    chunks = samples // LANES
    pairs = observed.shape[0]
    combos = CHANS * CHANS
    share = pairs // window_groups
    corr_scale = 1.0 / math.sqrt(samples * local_windows * window_groups)
    adj_scale = 1.0 / math.sqrt(CHANS * LAGS)

    chips = slots // 2
    block = jax.ShapeDtypeStruct((CHANS, chunks, LANES), jnp.bfloat16)
    blocks = jax.ShapeDtypeStruct((chips, CHANS, chunks, LANES), jnp.bfloat16)
    any_space = pl.BlockSpec(memory_space=pltpu.HBM)
    planes = jnp.transpose(records, (1, 2, 0, 3)).reshape(CHANS, stations, samples)
    planes = pltpu.with_memory_space_constraint(planes, pltpu.HBM)
    send_rows, pair_first, pair_second, lag_lo, lag_hi = [
        pltpu.with_memory_space_constraint(x, pltpu.HBM)
        for x in (send_rows, pair_first, pair_second, lag_lo, lag_hi)
    ]
    swap, *keep = pl.pallas_call(
        pack_kernel,
        in_specs=[smem(), any_space],
        out_specs=[vmem()] * (1 + chips),
        out_shape=[blocks] + [block] * chips,
        scratch_shapes=[
            pltpu.VMEM((CHANS, stations, samples), jnp.bfloat16),
            pltpu.VMEM((CHANS, chunks * stations, LANES), jnp.float32),
            pltpu.SemaphoreType.DMA((CHANS,)),
        ],
        compiler_params=pltpu.CompilerParams(vmem_limit_bytes=8 * 2**20),
        name="pack",
    )(send_rows, planes)
    order, arrived = across(swap, keep)

    rows = 3 * LANES - HALF_TILE
    corr, fan = pl.pallas_call(
        functools.partial(corr_kernel, order),
        in_specs=[any_space] * 2 + [vmem()] * (chips + 1),
        out_specs=[vmem(), vmem()],
        out_shape=[
            jax.ShapeDtypeStruct((combos, pairs, LAGS), jnp.float32),
            jax.ShapeDtypeStruct((slots * CHANS, rows, LANES), jnp.bfloat16),
        ],
        scratch_shapes=[
            pltpu.VMEM((slots, CHANS * WIDE, HALF_TILE // WIDE * LANES), jnp.bfloat16),
            pltpu.SMEM((pairs,), jnp.int32),
            pltpu.SMEM((pairs,), jnp.int32),
            pltpu.SemaphoreType.DMA((2,)),
        ],
        compiler_params=pltpu.CompilerParams(vmem_limit_bytes=16 * 2**20),
        name="corr",
    )(pair_first, pair_second, *arrived)
    parts = window_parts(corr)

    seen = jnp.transpose(observed, (1, 2, 0, 3)).reshape(combos, pairs, LAGS)
    *keep, swap, residual = pl.pallas_call(
        functools.partial(adjoint_kernel, corr_scale, adj_scale),
        in_specs=[any_space] * 4 + [vmem()] * (2 + len(parts)),
        out_specs=[vmem()] * (chips + 2),
        out_shape=[block] * chips
        + [blocks, jax.ShapeDtypeStruct((combos, share, LAGS), jnp.float32)],
        scratch_shapes=[
            pltpu.VMEM((combos, pairs, LAGS), jnp.float32),
            pltpu.VMEM((combos * pairs, WINDOW), jnp.float32),
            pltpu.VMEM((combos * pairs, WINDOW), jnp.float32),
            pltpu.VMEM((slots, slots * CHANS * PHASES, DEPTH), jnp.bfloat16),
            pltpu.VMEM((slots * CHANS * PHASES, 4 * LANES), jnp.float32),
            pltpu.SMEM((pairs,), jnp.int32),
            pltpu.SMEM((pairs,), jnp.int32),
            pltpu.SMEM((pairs,), jnp.int32),
            pltpu.SMEM((pairs,), jnp.int32),
            pltpu.SemaphoreType.DMA((4,)),
        ],
        compiler_params=pltpu.CompilerParams(vmem_limit_bytes=44 * 2**20),
        name="adjoint",
    )(
        pair_first, pair_second, lag_lo, lag_hi, seen, fan, *parts,
    )
    order, returned = across(swap, keep)
    stacked = pl.pallas_call(
        functools.partial(unpack_kernel, order),
        in_specs=[smem()] + [vmem()] * (chips + 1),
        out_specs=any_space,
        out_shape=jax.ShapeDtypeStruct((CHANS, stations, samples), jnp.bfloat16),
        scratch_shapes=[
            pltpu.VMEM((CHANS, stations, samples), jnp.bfloat16),
            pltpu.VMEM((CHANS, chunks * stations, LANES), jnp.float32),
            pltpu.SemaphoreType.DMA((CHANS,)),
        ],
        compiler_params=pltpu.CompilerParams(vmem_limit_bytes=8 * 2**20),
        name="unpack",
    )(send_rows, *returned)
    station_adjoint = jnp.transpose(stacked.reshape(1, CHANS, stations, samples), (2, 0, 1, 3))
    residual = jnp.transpose(residual.reshape(CHANS, CHANS, share, LAGS), (2, 0, 1, 3))
    return (station_adjoint, residual)


def solution(mesh):
    placed = (
        P("stn", "win", None, None),
        P("stn", None, None, None),
        P("stn"),
        P("stn"),
        P("stn", None, None),
        P("stn"),
        P("stn"),
    )
    return jax.shard_map(
        shards,
        mesh=mesh,
        in_specs=placed,
        out_specs=(P("stn", "win", None, None), P(("stn", "win"), None, None, None)),
        check_vma=False,
    )
```

```python
import functools
import math

import jax
import jax.numpy as jnp
from jax import lax
from jax.experimental import pallas as pl
from jax.experimental.pallas import tpu as pltpu
from jax.sharding import PartitionSpec as P

LAGS = 256
HALF = LAGS // 2
LANES = 128
HALF_TILE = LANES // 2
PHASES = 16
WIDE = 32
EARLY = 12
CHANS = 3
WINDOW = 3 * LANES
DEPTH = 7 * LANES


def fetch(sources, targets, sems):
    copies = [pltpu.make_async_copy(s, t, sems.at[k]) for k, (s, t) in enumerate(zip(sources, targets))]
    for copy in copies:
        copy.start()
    return copies


def pack_kernel(rows_in, rec_ref, swap_ref, *refs):
    keep_refs = refs[:-4]
    buffer, scratch, rows_ref, sems = refs[-4:]
    me = lax.axis_index("stn")
    stations = rec_ref.shape[1]
    chunks = rec_ref.shape[2] // LANES
    copies = fetch(
        [rows_in] + [rec_ref.at[c] for c in range(CHANS)],
        [rows_ref] + [buffer.at[c] for c in range(CHANS)],
        sems,
    )
    copies[0].wait()
    for c in range(CHANS):
        copies[c + 1].wait()
        for r in range(chunks):
            piece = buffer[c, :, r * LANES:(r + 1) * LANES]
            scratch[c, r * stations:(r + 1) * stations, :] = piece.astype(jnp.float32)
        for j, keep_ref in enumerate(keep_refs):
            for i, ref in enumerate((keep_ref, swap_ref.at[j])):
                station = rows_ref[me ^ (2 * j + i)]
                picked = scratch[c, pl.ds(station, chunks, stride=stations), :]
                ref[c] = picked.astype(jnp.bfloat16)


def unpack_kernel(order, rows_in, *refs):
    returned = refs[:-5]
    out_ref, buffer, scratch, rows_ref, sems = refs[-5:]
    rows_copy = pltpu.make_async_copy(rows_in, rows_ref, sems.at[CHANS])
    rows_copy.start()
    scratch[...] = jnp.zeros_like(scratch)
    rows_copy.wait()
    me = lax.axis_index("stn")
    stations = out_ref.shape[1]
    chunks = out_ref.shape[2] // LANES
    copies = []
    for c in range(CHANS):
        pieces = [(2 * j + i, ref.at[i]) for j, ref in zip(order, returned[:-2]) for i in range(2)]
        for j, ref in pieces + [(0, returned[-2]), (1, returned[-1])]:
            where = pl.ds(rows_ref[me ^ j], chunks, stride=stations)
            scratch[c, where, :] = scratch[c, where, :] + ref[c].astype(jnp.float32)
        for r in range(chunks):
            piece = scratch[c, r * stations:(r + 1) * stations, :]
            buffer[c, :, r * LANES:(r + 1) * LANES] = piece.astype(jnp.bfloat16)
        copies.append(pltpu.make_async_copy(buffer.at[c], out_ref.at[c], sems.at[c]))
        copies[c].start()
    for copy in copies:
        copy.wait()


def build_phases(slot_refs, fan_ref):
    chunks = slot_refs[0].shape[1]
    rows = fan_ref.shape[1]
    lane = lax.broadcasted_iota(jnp.int32, (LANES, LANES), 1)
    left = lax.broadcasted_iota(jnp.int32, (rows, LANES), 1) < chunks
    for place in range(0, CHANS * len(slot_refs), 2):
        pair = [slot_refs[e // CHANS][e % CHANS] for e in (place, place + 1)]
        middle = jnp.concatenate(pair, axis=0).astype(jnp.float32).T
        before = jnp.where(lane % chunks == 0, 0.0, pltpu.roll(middle, 1, 1))
        after = jnp.where(lane % chunks == chunks - 1, 0.0, pltpu.roll(middle, LANES - 1, 1))
        wide = jnp.concatenate([before, middle, after], axis=0)
        swapped = pltpu.roll(wide, chunks, 1)
        one = jnp.where(left, wide[:rows], swapped[HALF_TILE:])
        two = jnp.where(left, swapped[:rows], wide[HALF_TILE:])
        fan_ref[place] = one.astype(jnp.bfloat16)
        fan_ref[place + 1] = two.astype(jnp.bfloat16)


def shifted_rows(fan_ref, slot, phases):
    span = LAGS + phases
    tail = DEPTH - CHANS * span
    columns = []
    for first in range(0, HALF_TILE, phases):
        parts = [fan_ref[CHANS * slot + b, first:first + span, :] for b in range(CHANS)]
        parts.append(fan_ref[CHANS * slot, first:first + tail, :])
        columns.append(jnp.concatenate(parts, axis=0))
    return jnp.concatenate(columns, axis=1)


def prep_kernel(
    token, first_in, second_in, rows_in, low_in, high_in, observed_in,
    bands, first_out, second_out, rows_out, inside, seen, seen_later,
    staged, low_ref, high_ref, sems,
):
    copies = fetch(
        (low_in, high_in, observed_in, first_in, second_in, rows_in),
        (low_ref, high_ref, staged, first_out, second_out, rows_out),
        sems,
    )
    bands[...] = jnp.zeros_like(bands)
    for copy in copies:
        copy.wait()
    pairs = inside.shape[0]
    early = seen.shape[1]
    row = lax.broadcasted_iota(jnp.int32, (pairs, LAGS), 0)
    lag = lax.broadcasted_iota(jnp.int32, (pairs, LAGS), 1)
    low = jnp.zeros_like(row)
    high = jnp.zeros_like(row)
    for p in range(pairs):
        low = jnp.where(row == p, low_ref[p], low)
        high = jnp.where(row == p, high_ref[p], high)
    inside[...] = ((lag >= low) & (lag < high)).astype(jnp.int32)
    for i in range(seen.shape[0]):
        seen[i] = staged[i, :early]
        seen_later[i] = staged[i, early:]


def correlate(start, first_ref, second_ref, fan_ref, heads, corr_ref):
    me = lax.axis_index("stn")

    def step(p, carry):
        right = shifted_rows(fan_ref, second_ref[start + p] ^ me, WIDE)
        products = lax.dot_general(
            heads[first_ref[start + p] ^ me], right, (((1,), (1,)), ((), ())),
            preferred_element_type=jnp.float32,
        )
        for a in range(CHANS):
            for b in range(CHANS):
                block = products[WIDE * a:WIDE * (a + 1), LAGS * b:LAGS * b + WINDOW]
                shift = WINDOW - WIDE * b - (WIDE - 1)
                turned = pltpu.roll(block, shift, 1, stride=1, stride_axis=0)
                corr_ref[CHANS * a + b, pl.ds(p, 1), :] = jnp.sum(
                    turned[:, :LAGS], axis=0, keepdims=True
                )
        return carry

    count = corr_ref.shape[1]
    lax.fori_loop(0, count, step, 0, unroll=min(count, 16))


def corr_first_kernel(order, first_in, second_in, *refs):
    given = refs[:-6]
    corr_ref, fan_ref, heads, first_ref, second_ref, sems = refs[-6:]
    copies = fetch((first_in, second_in), (first_ref, second_ref), sems)
    slot_refs = [None] * (2 * len(given) - 2)
    for j, ref in zip(order, given[:-2]):
        slot_refs[2 * j:2 * j + 2] = [ref.at[0], ref.at[1]]
    slot_refs[:2] = given[-2:]
    build_phases(slot_refs, fan_ref)
    height = CHANS * WIDE
    row = lax.broadcasted_iota(jnp.int32, (height, height), 0)
    column = lax.broadcasted_iota(jnp.int32, (height, height), 1)
    same = row // WIDE == column // WIDE
    flip = (same & (row % WIDE + column % WIDE == WIDE - 1)).astype(jnp.bfloat16)

    def head(q, carry):
        rows = []
        for a in range(CHANS):
            pieces = []
            for m in range(0, HALF_TILE, WIDE):
                pieces.append(fan_ref[CHANS * q + a, HALF + m:HALF + m + WIDE, :])
            rows.append(jnp.concatenate(pieces, axis=1))
        natural = jnp.concatenate(rows, axis=0)
        heads[q] = jnp.dot(flip, natural, preferred_element_type=jnp.float32).astype(jnp.bfloat16)
        return carry

    lax.fori_loop(0, heads.shape[0], head, 0, unroll=8)
    for copy in copies:
        copy.wait()
    correlate(0, first_ref, second_ref, fan_ref, heads, corr_ref)


def corr_second_kernel(start, first_ref, second_ref, fan_ref, heads, corr_ref):
    correlate(start, first_ref, second_ref, fan_ref, heads, corr_ref)


def spread(lag_rows, combos, p):
    turned = []
    for c, combo in enumerate(combos):
        block = jnp.broadcast_to(lag_rows[combo, pl.ds(p, 1), :], (PHASES, WINDOW))
        turned.append(pltpu.roll(block, PHASES * c, 1, stride=1, stride_axis=0))
    w0, w1, w2 = turned
    return jnp.concatenate(
        [
            w0[:, :LAGS],
            w0[:, LAGS:] + w1[:, :LANES],
            w1[:, LANES:LAGS],
            w1[:, LAGS:] + w2[:, :LANES],
            w2[:, LANES:],
        ],
        axis=1,
    ).astype(jnp.bfloat16)


def pairwise(terms):
    while len(terms) > 1:
        terms = [sum(terms[k + 1:k + 2], terms[k]) for k in range(0, len(terms), 2)]
    return terms[0]


def residuals(corr_scale, part_refs, observed_ref, inside, resid, forward, backward):
    combos, pairs, _ = resid.shape
    flip = (
        lax.broadcasted_iota(jnp.int32, (LAGS, WINDOW), 0)
        + lax.broadcasted_iota(jnp.int32, (LAGS, WINDOW), 1)
        == LAGS
    ).astype(jnp.bfloat16)
    forward[:, :, LAGS:] = jnp.zeros((combos, pairs, WINDOW - LAGS), jnp.float32)
    for i in range(combos):
        summed = pairwise([ref[i] for ref in part_refs])
        value = jnp.where(inside, summed * corr_scale - observed_ref[i], 0.0)
        resid[i] = value
        rounded = value.astype(jnp.bfloat16)
        forward[i, :, :LAGS] = rounded.astype(jnp.float32)
        backward[i] = jnp.dot(rounded, flip, preferred_element_type=jnp.float32)


def fill_bands(start, first_ref, second_ref, forward, backward, bands):
    me = lax.axis_index("stn")
    slots = bands.shape[0]
    pairs = forward.shape[1]
    height = CHANS * PHASES

    def row_place(q):
        return q // 2 + (slots // 2) * (1 - q % 2)

    def fill(p, carry):
        qf = first_ref[start + p] ^ me
        qs = second_ref[start + p] ^ me
        for c in range(CHANS):
            at = pl.multiple_of(height * row_place(qf) + PHASES * c, PHASES)
            bands[qs, pl.ds(at, PHASES), :] = spread(
                forward, [CHANS * c + b for b in range(CHANS)], p
            )
            at = pl.multiple_of(height * row_place(qs) + PHASES * c, PHASES)
            bands[qf, pl.ds(at, PHASES), :] = spread(
                backward, [CHANS * a + c for a in range(CHANS)], p
            )
        return carry

    lax.fori_loop(0, pairs, fill, 0, unroll=min(pairs, 16))


def contract(adj_scale, first_row, bands, fan_ref, total, outs):
    rows = total.shape[0]
    total[...] = jnp.zeros_like(total)

    def accumulate(r, carry):
        right = shifted_rows(fan_ref, r, PHASES)
        left = bands[r, first_row:first_row + rows, :]
        total[...] += jnp.dot(left, right, preferred_element_type=jnp.float32)
        return carry

    lax.fori_loop(0, bands.shape[0], accumulate, 0, unroll=8)
    chunks = outs[0].shape[1]
    near = lax.broadcasted_iota(jnp.int32, (PHASES, LANES), 1) < chunks
    for place in range(0, rows // PHASES, 2):
        upper = []
        lower = []
        for m in range(4):
            columns = slice(m * LANES, (m + 1) * LANES)
            one = total[place * PHASES:(place + 1) * PHASES, columns]
            two = total[(place + 1) * PHASES:(place + 2) * PHASES, columns]
            upper.append(jnp.where(near, one, pltpu.roll(two, chunks, 1)))
            lower.append(jnp.where(near, pltpu.roll(one, chunks, 1), two))
        tile = (jnp.concatenate(upper + lower, axis=0).T * adj_scale).astype(jnp.bfloat16)
        for k in range(2):
            e = place + k
            outs[e // CHANS][e % CHANS] = tile[k * chunks:(k + 1) * chunks]


def bands_kernel(corr_scale, first_in, second_in, inside_ref, seen_ref, bands_in, *refs):
    part_refs = refs[:-7]
    bands, resid, forward, backward, first_ref, second_ref, sems = refs[-7:]
    copies = fetch((first_in, second_in), (first_ref, second_ref), sems)
    inside = inside_ref[:resid.shape[1], :] > 0
    residuals(corr_scale, part_refs, seen_ref, inside, resid, forward, backward)
    for copy in copies:
        copy.wait()
    fill_bands(0, first_ref, second_ref, forward, backward, bands)


def adjoint_kernel(
    corr_scale, adj_scale, first_in, second_in, inside_ref, seen_ref, bands_in, fan_ref,
    earlier, *refs
):
    (bands, swap_ref, share_ref, resid, forward, backward, total,
     first_ref, second_ref, sems) = refs[-10:]
    part_refs = refs[:-10]
    copies = fetch((first_in, second_in), (first_ref, second_ref), sems)
    half = earlier.shape[1]
    inside = inside_ref[half:, :] > 0
    residuals(corr_scale, part_refs, seen_ref, inside, resid, forward, backward)
    offset = lax.axis_index("win") * share_ref.shape[1]
    for j in range(share_ref.shape[1]):
        p = offset + j
        for i in range(resid.shape[0]):
            one = earlier[i, pl.ds(jnp.minimum(p, half - 1), 1), :]
            two = resid[i, pl.ds(jnp.maximum(p - half, 0), 1), :]
            share_ref[i, j:j + 1, :] = jnp.where(p < half, one, two)
    for copy in copies:
        copy.wait()
    fill_bands(half, first_ref, second_ref, forward, backward, bands)
    outs = [swap_ref.at[j] for j in range(swap_ref.shape[0])]
    contract(adj_scale, 0, bands, fan_ref, total, outs)


def keep_kernel(adj_scale, bands, fan_ref, *refs):
    outs = refs[:-1]
    total = refs[-1]
    contract(adj_scale, total.shape[0], bands, fan_ref, total, outs)


def smem():
    return pl.BlockSpec(memory_space=pltpu.SMEM)


def vmem():
    return pl.BlockSpec(memory_space=pltpu.VMEM)


def flipped(x, axis, bits):
    count = lax.axis_size(axis)
    return lax.ppermute(x, axis, [(k, k ^ bits) for k in range(count)])


def across(swap, keep):
    chips = len(keep)
    got = flipped(swap, "stn", 1)
    order = []
    blocks = []
    for j in range(chips - 1, 0, -1):
        moved = flipped(jnp.stack([keep[j], got[j]]), "stn", 2 * j)
        order.append(j)
        blocks.append(moved)
    return order + [0, 0], blocks + [keep[0], got[0]]


def window_parts(corr):
    groups = lax.axis_size("win")
    if groups > 4:
        gathered = lax.all_gather(corr, "win")
        return [gathered[w] for w in range(groups)]
    return [corr] + [flipped(corr, "win", w) for w in range(1, groups)]


def shards(records, observed, lag_lo, lag_hi, send_table, pair_first, pair_second):
    owner_count = lax.axis_size("stn")
    window_groups = lax.axis_size("win")
    stations, local_windows, _, samples = records.shape
    send_rows = send_table.reshape(-1)
    slots = send_rows.shape[0]
    chunks = samples // LANES
    pairs = observed.shape[0]
    combos = CHANS * CHANS
    share = pairs // window_groups
    corr_scale = 1.0 / math.sqrt(samples * local_windows * window_groups)
    adj_scale = 1.0 / math.sqrt(CHANS * LAGS)

    chips = slots // 2
    block = jax.ShapeDtypeStruct((CHANS, chunks, LANES), jnp.bfloat16)
    blocks = jax.ShapeDtypeStruct((chips, CHANS, chunks, LANES), jnp.bfloat16)
    any_space = pl.BlockSpec(memory_space=pltpu.HBM)
    planes = jnp.transpose(records, (1, 2, 0, 3)).reshape(CHANS, stations, samples)
    planes = pltpu.with_memory_space_constraint(planes, pltpu.HBM)
    send_rows, pair_first, pair_second, lag_lo, lag_hi = [
        pltpu.with_memory_space_constraint(x, pltpu.HBM)
        for x in (send_rows, pair_first, pair_second, lag_lo, lag_hi)
    ]
    swap, *keep = pl.pallas_call(
        pack_kernel,
        in_specs=[any_space, any_space],
        out_specs=[vmem()] * (1 + chips),
        out_shape=[blocks] + [block] * chips,
        scratch_shapes=[
            pltpu.VMEM((CHANS, stations, samples), jnp.bfloat16),
            pltpu.VMEM((CHANS, chunks * stations, LANES), jnp.float32),
            pltpu.SMEM((slots,), jnp.int32),
            pltpu.SemaphoreType.DMA((CHANS + 1,)),
        ],
        compiler_params=pltpu.CompilerParams(vmem_limit_bytes=8 * 2**20),
        name="pack",
    )(send_rows, planes)
    rows = 3 * LANES - HALF_TILE
    early = pairs * EARLY // 16
    fan_shape = jax.ShapeDtypeStruct((slots * CHANS, rows, LANES), jnp.bfloat16)
    corr_shape = jax.ShapeDtypeStruct((combos, early, LAGS), jnp.float32)
    late_shape = jax.ShapeDtypeStruct((combos, pairs - early, LAGS), jnp.float32)
    index_shape = jax.ShapeDtypeStruct((pairs,), jnp.int32)
    height = slots * CHANS * PHASES
    bands_shape = jax.ShapeDtypeStruct((slots, height, DEPTH), jnp.bfloat16)
    index_scratch = pltpu.SMEM((pairs,), jnp.int32)
    small = pltpu.CompilerParams(vmem_limit_bytes=16 * 2**20)
    cost = pl.CostEstimate(flops=2 * 10**9, bytes_accessed=2**22, transcendentals=0)
    seen = jnp.transpose(observed, (1, 2, 0, 3)).reshape(combos, pairs, LAGS)
    seen = pltpu.with_memory_space_constraint(seen, pltpu.HBM)
    bands, firsts, seconds, rows_copy, inside, seen, seen_later = pl.pallas_call(
        prep_kernel,
        in_specs=[pl.BlockSpec(memory_space=pl.ANY)] + [any_space] * 6,
        out_specs=[vmem()] * 7,
        out_shape=[
            bands_shape,
            index_shape,
            index_shape,
            jax.ShapeDtypeStruct((slots,), jnp.int32),
            jax.ShapeDtypeStruct((pairs, LAGS), jnp.int32),
            corr_shape,
            late_shape,
        ],
        scratch_shapes=[
            pltpu.VMEM((combos, pairs, LAGS), jnp.float32),
            index_scratch,
            index_scratch,
            pltpu.SemaphoreType.DMA((6,)),
        ],
        compiler_params=small,
        cost_estimate=cost,
        name="prep",
    )(swap, pair_first, pair_second, send_rows, lag_lo, lag_hi, seen)
    order, arrived = across(swap, keep)

    corr, fan, heads = pl.pallas_call(
        functools.partial(corr_first_kernel, order),
        in_specs=[vmem()] * (chips + 3),
        out_specs=[vmem()] * 3,
        out_shape=[
            corr_shape,
            fan_shape,
            jax.ShapeDtypeStruct(
                (slots, CHANS * WIDE, HALF_TILE // WIDE * LANES), jnp.bfloat16
            ),
        ],
        scratch_shapes=[index_scratch, index_scratch, pltpu.SemaphoreType.DMA((2,))],
        compiler_params=small,
        cost_estimate=cost,
        name="corr_first",
    )(firsts, seconds, *arrived)
    parts = window_parts(corr)
    later = pl.pallas_call(
        functools.partial(corr_second_kernel, early),
        in_specs=[smem(), smem(), vmem(), vmem()],
        out_specs=vmem(),
        out_shape=late_shape,
        compiler_params=small,
        cost_estimate=cost,
        name="corr_second",
    )(firsts, seconds, fan, heads)
    later_parts = window_parts(later)

    lag_rows = pltpu.VMEM((combos, early, WINDOW), jnp.float32)
    bands, resid = pl.pallas_call(
        functools.partial(bands_kernel, corr_scale),
        in_specs=[vmem()] * (5 + len(parts)),
        out_specs=[vmem()] * 2,
        out_shape=[bands_shape, corr_shape],
        scratch_shapes=[
            lag_rows, lag_rows, index_scratch, index_scratch, pltpu.SemaphoreType.DMA((2,))
        ],
        input_output_aliases={4: 0},
        compiler_params=small,
        cost_estimate=cost,
        name="bands",
    )(firsts, seconds, inside, seen, bands, *parts)
    total = pltpu.VMEM((height // 2, 4 * LANES), jnp.float32)
    lag_rows = pltpu.VMEM((combos, pairs - early, WINDOW), jnp.float32)
    bands, swap, residual = pl.pallas_call(
        functools.partial(adjoint_kernel, corr_scale, adj_scale),
        in_specs=[vmem()] * (7 + len(later_parts)),
        out_specs=[vmem()] * 3,
        out_shape=[bands_shape, blocks, jax.ShapeDtypeStruct((combos, share, LAGS), jnp.float32)],
        scratch_shapes=[
            pltpu.VMEM((combos, pairs - early, LAGS), jnp.float32),
            lag_rows,
            lag_rows,
            total,
            index_scratch,
            index_scratch,
            pltpu.SemaphoreType.DMA((2,)),
        ],
        input_output_aliases={4: 0},
        compiler_params=small,
        cost_estimate=cost,
        name="adjoint",
    )(firsts, seconds, inside, seen_later, bands, fan, resid, *later_parts)
    keep = pl.pallas_call(
        functools.partial(keep_kernel, adj_scale),
        in_specs=[vmem()] * 2,
        out_specs=[vmem()] * chips,
        out_shape=[block] * chips,
        scratch_shapes=[total],
        compiler_params=small,
        cost_estimate=cost,
        name="keep",
    )(bands, fan)
    order, returned = across(swap, keep)
    stacked = pl.pallas_call(
        functools.partial(unpack_kernel, order),
        in_specs=[vmem()] * (chips + 2),
        out_specs=any_space,
        out_shape=jax.ShapeDtypeStruct((CHANS, stations, samples), jnp.bfloat16),
        scratch_shapes=[
            pltpu.VMEM((CHANS, stations, samples), jnp.bfloat16),
            pltpu.VMEM((CHANS, chunks * stations, LANES), jnp.float32),
            pltpu.SMEM((slots,), jnp.int32),
            pltpu.SemaphoreType.DMA((CHANS + 1,)),
        ],
        compiler_params=pltpu.CompilerParams(vmem_limit_bytes=8 * 2**20),
        name="unpack",
    )(rows_copy, *returned)
    station_adjoint = jnp.transpose(stacked.reshape(1, CHANS, stations, samples), (2, 0, 1, 3))
    residual = jnp.transpose(residual.reshape(CHANS, CHANS, share, LAGS), (2, 0, 1, 3))
    return (station_adjoint, residual)


def solution(mesh):
    placed = (
        P("stn", "win", None, None),
        P("stn", None, None, None),
        P("stn"),
        P("stn"),
        P("stn", None, None),
        P("stn"),
        P("stn"),
    )
    return jax.shard_map(
        shards,
        mesh=mesh,
        in_specs=placed,
        out_specs=(P("stn", "win", None, None), P(("stn", "win"), None, None, None)),
        check_vma=False,
    )
```

```python
import functools
import math

import jax
import jax.numpy as jnp
from jax import lax
from jax.experimental import pallas as pl
from jax.experimental.pallas import tpu as pltpu
from jax.sharding import PartitionSpec as P

LAGS = 256
HALF = LAGS // 2
LANES = 128
HALF_TILE = LANES // 2
PHASES = 16
WIDE = 32
EARLY = 14
CHANS = 3
WINDOW = 3 * LANES
DEPTH = 7 * LANES


def member(me, chips, step, other):
    return 2 * ((me // 2 + step) & (chips - 1)) + ((me & 1) ^ other)


def near_slot(q, me, chips):
    return 2 * ((me // 2 - q // 2) & (chips - 1)) + ((q ^ me) & 1)


def fetch(sources, targets, sems):
    copies = [pltpu.make_async_copy(s, t, sems.at[k]) for k, (s, t) in enumerate(zip(sources, targets))]
    for copy in copies:
        copy.start()
    return copies


def pack_kernel(rows_in, rec_ref, swap_ref, *refs):
    keep_refs = refs[:-4]
    buffer, scratch, rows_ref, sems = refs[-4:]
    me = lax.axis_index("stn")
    stations = rec_ref.shape[1]
    chunks = rec_ref.shape[2] // LANES
    copies = fetch(
        [rows_in] + [rec_ref.at[c] for c in range(CHANS)],
        [rows_ref] + [buffer.at[c] for c in range(CHANS)],
        sems,
    )
    copies[0].wait()
    for c in range(CHANS):
        copies[c + 1].wait()
        for r in range(chunks):
            piece = buffer[c, :, r * LANES:(r + 1) * LANES]
            scratch[c, r * stations:(r + 1) * stations, :] = piece.astype(jnp.float32)
        for j, keep_ref in enumerate(keep_refs):
            for i, ref in enumerate((keep_ref, swap_ref.at[j])):
                station = rows_ref[member(me, len(keep_refs), j, i)]
                picked = scratch[c, pl.ds(station, chunks, stride=stations), :]
                ref[c] = picked.astype(jnp.bfloat16)


def unpack_kernel(order, rows_in, *refs):
    returned = refs[:-5]
    out_ref, buffer, scratch, rows_ref, sems = refs[-5:]
    rows_copy = pltpu.make_async_copy(rows_in, rows_ref, sems.at[CHANS])
    rows_copy.start()
    scratch[...] = jnp.zeros_like(scratch)
    rows_copy.wait()
    me = lax.axis_index("stn")
    stations = out_ref.shape[1]
    chunks = out_ref.shape[2] // LANES
    copies = []
    for c in range(CHANS):
        pieces = [(2 * j + i, ref.at[i]) for j, ref in zip(order, returned[:-2]) for i in range(2)]
        for j, ref in pieces + [(0, returned[-2]), (1, returned[-1])]:
            station = rows_ref[member(me, len(order) - 1, j // 2, j % 2)]
            where = pl.ds(station, chunks, stride=stations)
            scratch[c, where, :] = scratch[c, where, :] + ref[c].astype(jnp.float32)
        for r in range(chunks):
            piece = scratch[c, r * stations:(r + 1) * stations, :]
            buffer[c, :, r * LANES:(r + 1) * LANES] = piece.astype(jnp.bfloat16)
        copies.append(pltpu.make_async_copy(buffer.at[c], out_ref.at[c], sems.at[c]))
        copies[c].start()
    for copy in copies:
        copy.wait()


def build_phases(slot_refs, fan_ref):
    chunks = slot_refs[0].shape[1]
    rows = fan_ref.shape[1]
    lane = lax.broadcasted_iota(jnp.int32, (LANES, LANES), 1)
    left = lax.broadcasted_iota(jnp.int32, (rows, LANES), 1) < chunks
    for place in range(0, CHANS * len(slot_refs), 2):
        pair = [slot_refs[e // CHANS][e % CHANS] for e in (place, place + 1)]
        middle = jnp.concatenate(pair, axis=0).astype(jnp.float32).T
        before = jnp.where(lane % chunks == 0, 0.0, pltpu.roll(middle, 1, 1))
        after = jnp.where(lane % chunks == chunks - 1, 0.0, pltpu.roll(middle, LANES - 1, 1))
        wide = jnp.concatenate([before, middle, after], axis=0)
        swapped = pltpu.roll(wide, chunks, 1)
        one = jnp.where(left, wide[:rows], swapped[HALF_TILE:])
        two = jnp.where(left, swapped[:rows], wide[HALF_TILE:])
        fan_ref[place] = one.astype(jnp.bfloat16)
        fan_ref[place + 1] = two.astype(jnp.bfloat16)


def shifted_rows(fan_ref, slot, phases):
    span = LAGS + phases
    tail = DEPTH - CHANS * span
    columns = []
    for first in range(0, HALF_TILE, phases):
        parts = [fan_ref[CHANS * slot + b, first:first + span, :] for b in range(CHANS)]
        parts.append(fan_ref[CHANS * slot, first:first + tail, :])
        columns.append(jnp.concatenate(parts, axis=0))
    return jnp.concatenate(columns, axis=1)


def prep_kernel(
    token, first_in, second_in, rows_in, low_in, high_in, observed_in,
    bands, first_out, second_out, rows_out, inside, seen, seen_later,
    staged, low_ref, high_ref, sems,
):
    copies = fetch(
        (low_in, high_in, observed_in, first_in, second_in, rows_in),
        (low_ref, high_ref, staged, first_out, second_out, rows_out),
        sems,
    )
    bands[...] = jnp.zeros_like(bands)
    for copy in copies:
        copy.wait()
    pairs = inside.shape[0]
    early = seen.shape[1]
    row = lax.broadcasted_iota(jnp.int32, (pairs, LAGS), 0)
    lag = lax.broadcasted_iota(jnp.int32, (pairs, LAGS), 1)
    low = jnp.zeros_like(row)
    high = jnp.zeros_like(row)
    for p in range(pairs):
        low = jnp.where(row == p, low_ref[p], low)
        high = jnp.where(row == p, high_ref[p], high)
    inside[...] = ((lag >= low) & (lag < high)).astype(jnp.int32)
    for i in range(seen.shape[0]):
        seen[i] = staged[i, :early]
        seen_later[i] = staged[i, early:]


def correlate(start, first_ref, second_ref, fan_ref, heads, corr_ref):
    me = lax.axis_index("stn")
    chips = heads.shape[0] // 2

    def step(p, carry):
        right = shifted_rows(fan_ref, near_slot(second_ref[start + p], me, chips), WIDE)
        products = lax.dot_general(
            heads[near_slot(first_ref[start + p], me, chips)], right, (((1,), (1,)), ((), ())),
            preferred_element_type=jnp.float32,
        )
        for a in range(CHANS):
            for b in range(CHANS):
                block = products[WIDE * a:WIDE * (a + 1), LAGS * b:LAGS * b + WINDOW]
                shift = WINDOW - WIDE * b - (WIDE - 1)
                turned = pltpu.roll(block, shift, 1, stride=1, stride_axis=0)
                corr_ref[CHANS * a + b, pl.ds(p, 1), :] = jnp.sum(
                    turned[:, :LAGS], axis=0, keepdims=True
                )
        return carry

    count = corr_ref.shape[1]
    lax.fori_loop(0, count, step, 0, unroll=min(count, 16))


def corr_first_kernel(order, first_in, second_in, *refs):
    given = refs[:-6]
    corr_ref, fan_ref, heads, first_ref, second_ref, sems = refs[-6:]
    copies = fetch((first_in, second_in), (first_ref, second_ref), sems)
    slot_refs = [None] * (2 * len(given) - 2)
    for j, ref in zip(order, given[:-2]):
        slot_refs[2 * j:2 * j + 2] = [ref.at[0], ref.at[1]]
    slot_refs[:2] = given[-2:]
    build_phases(slot_refs, fan_ref)
    height = CHANS * WIDE
    row = lax.broadcasted_iota(jnp.int32, (height, height), 0)
    column = lax.broadcasted_iota(jnp.int32, (height, height), 1)
    same = row // WIDE == column // WIDE
    flip = (same & (row % WIDE + column % WIDE == WIDE - 1)).astype(jnp.bfloat16)

    def head(q, carry):
        rows = []
        for a in range(CHANS):
            pieces = []
            for m in range(0, HALF_TILE, WIDE):
                pieces.append(fan_ref[CHANS * q + a, HALF + m:HALF + m + WIDE, :])
            rows.append(jnp.concatenate(pieces, axis=1))
        natural = jnp.concatenate(rows, axis=0)
        heads[q] = jnp.dot(flip, natural, preferred_element_type=jnp.float32).astype(jnp.bfloat16)
        return carry

    lax.fori_loop(0, heads.shape[0], head, 0, unroll=8)
    for copy in copies:
        copy.wait()
    correlate(0, first_ref, second_ref, fan_ref, heads, corr_ref)


def corr_second_kernel(start, first_ref, second_ref, fan_ref, heads, corr_ref):
    correlate(start, first_ref, second_ref, fan_ref, heads, corr_ref)


def spread(lag_rows, combos, p):
    turned = []
    for c, combo in enumerate(combos):
        block = jnp.broadcast_to(lag_rows[combo, pl.ds(p, 1), :], (PHASES, WINDOW))
        turned.append(pltpu.roll(block, PHASES * c, 1, stride=1, stride_axis=0))
    w0, w1, w2 = turned
    return jnp.concatenate(
        [
            w0[:, :LAGS],
            w0[:, LAGS:] + w1[:, :LANES],
            w1[:, LANES:LAGS],
            w1[:, LAGS:] + w2[:, :LANES],
            w2[:, LANES:],
        ],
        axis=1,
    ).astype(jnp.bfloat16)


def pairwise(terms):
    while len(terms) > 1:
        terms = [sum(terms[k + 1:k + 2], terms[k]) for k in range(0, len(terms), 2)]
    return terms[0]


def residuals(corr_scale, part_refs, observed_ref, inside, resid, forward, backward):
    combos, pairs, _ = resid.shape
    flip = (
        lax.broadcasted_iota(jnp.int32, (LAGS, WINDOW), 0)
        + lax.broadcasted_iota(jnp.int32, (LAGS, WINDOW), 1)
        == LAGS
    ).astype(jnp.bfloat16)
    forward[:, :, LAGS:] = jnp.zeros((combos, pairs, WINDOW - LAGS), jnp.float32)
    for i in range(combos):
        summed = pairwise([ref[i] for ref in part_refs])
        value = jnp.where(inside, summed * corr_scale - observed_ref[i], 0.0)
        resid[i] = value
        rounded = value.astype(jnp.bfloat16)
        forward[i, :, :LAGS] = rounded.astype(jnp.float32)
        backward[i] = jnp.dot(rounded, flip, preferred_element_type=jnp.float32)


def fill_bands(start, first_ref, second_ref, forward, backward, bands):
    me = lax.axis_index("stn")
    slots = bands.shape[0]
    pairs = forward.shape[1]
    height = CHANS * PHASES

    def row_place(q):
        return q // 2 + (slots // 2) * (1 - q % 2)

    def fill(p, carry):
        qf = near_slot(first_ref[start + p], me, slots // 2)
        qs = near_slot(second_ref[start + p], me, slots // 2)
        for c in range(CHANS):
            at = pl.multiple_of(height * row_place(qf) + PHASES * c, PHASES)
            bands[qs, pl.ds(at, PHASES), :] = spread(
                forward, [CHANS * c + b for b in range(CHANS)], p
            )
            at = pl.multiple_of(height * row_place(qs) + PHASES * c, PHASES)
            bands[qf, pl.ds(at, PHASES), :] = spread(
                backward, [CHANS * a + c for a in range(CHANS)], p
            )
        return carry

    lax.fori_loop(0, pairs, fill, 0, unroll=min(pairs, 16))


def contract(adj_scale, first_row, bands, fan_ref, total, outs):
    rows = total.shape[0]
    total[...] = jnp.zeros_like(total)

    def accumulate(r, carry):
        right = shifted_rows(fan_ref, r, PHASES)
        left = bands[r, first_row:first_row + rows, :]
        total[...] += jnp.dot(left, right, preferred_element_type=jnp.float32)
        return carry

    lax.fori_loop(0, bands.shape[0], accumulate, 0, unroll=8)
    chunks = outs[0].shape[1]
    near = lax.broadcasted_iota(jnp.int32, (PHASES, LANES), 1) < chunks
    for place in range(0, rows // PHASES, 2):
        upper = []
        lower = []
        for m in range(4):
            columns = slice(m * LANES, (m + 1) * LANES)
            one = total[place * PHASES:(place + 1) * PHASES, columns]
            two = total[(place + 1) * PHASES:(place + 2) * PHASES, columns]
            upper.append(jnp.where(near, one, pltpu.roll(two, chunks, 1)))
            lower.append(jnp.where(near, pltpu.roll(one, chunks, 1), two))
        tile = (jnp.concatenate(upper + lower, axis=0).T * adj_scale).astype(jnp.bfloat16)
        for k in range(2):
            e = place + k
            outs[e // CHANS][e % CHANS] = tile[k * chunks:(k + 1) * chunks]


def bands_kernel(corr_scale, first_in, second_in, inside_ref, seen_ref, bands_in, *refs):
    part_refs = refs[:-7]
    bands, resid, forward, backward, first_ref, second_ref, sems = refs[-7:]
    copies = fetch((first_in, second_in), (first_ref, second_ref), sems)
    inside = inside_ref[:resid.shape[1], :] > 0
    residuals(corr_scale, part_refs, seen_ref, inside, resid, forward, backward)
    for copy in copies:
        copy.wait()
    fill_bands(0, first_ref, second_ref, forward, backward, bands)


def adjoint_kernel(
    corr_scale, adj_scale, first_in, second_in, inside_ref, seen_ref, bands_in, fan_ref,
    earlier, *refs
):
    (bands, swap_ref, share_ref, resid, forward, backward, total,
     first_ref, second_ref, sems) = refs[-10:]
    part_refs = refs[:-10]
    copies = fetch((first_in, second_in), (first_ref, second_ref), sems)
    half = earlier.shape[1]
    inside = inside_ref[half:, :] > 0
    residuals(corr_scale, part_refs, seen_ref, inside, resid, forward, backward)
    offset = lax.axis_index("win") * share_ref.shape[1]
    for j in range(share_ref.shape[1]):
        p = offset + j
        for i in range(resid.shape[0]):
            one = earlier[i, pl.ds(jnp.minimum(p, half - 1), 1), :]
            two = resid[i, pl.ds(jnp.maximum(p - half, 0), 1), :]
            share_ref[i, j:j + 1, :] = jnp.where(p < half, one, two)
    for copy in copies:
        copy.wait()
    fill_bands(half, first_ref, second_ref, forward, backward, bands)
    outs = [swap_ref.at[j] for j in range(swap_ref.shape[0])]
    contract(adj_scale, 0, bands, fan_ref, total, outs)


def keep_kernel(adj_scale, bands, fan_ref, *refs):
    outs = refs[:-1]
    total = refs[-1]
    contract(adj_scale, total.shape[0], bands, fan_ref, total, outs)


def smem():
    return pl.BlockSpec(memory_space=pltpu.SMEM)


def vmem():
    return pl.BlockSpec(memory_space=pltpu.VMEM)


def flipped(x, axis, bits):
    count = lax.axis_size(axis)
    return lax.ppermute(x, axis, [(k, k ^ bits) for k in range(count)])


def across(swap, keep, sign, first):
    chips = len(keep)
    got = flipped(swap, "stn", 1)
    order = first(chips)
    blocks = []
    for j in order:
        pairs = [(k, (k + 2 * sign * j) % (2 * chips)) for k in range(2 * chips)]
        blocks.append(lax.ppermute(jnp.stack([keep[j], got[j]]), "stn", pairs))
    return order + [0, 0], blocks + [keep[0], got[0]]


def window_parts(corr):
    groups = lax.axis_size("win")
    if groups > 4:
        gathered = lax.all_gather(corr, "win")
        return [gathered[w] for w in range(groups)]
    return [corr] + [flipped(corr, "win", w) for w in range(1, groups)]


def shards(records, observed, lag_lo, lag_hi, send_table, pair_first, pair_second):
    owner_count = lax.axis_size("stn")
    window_groups = lax.axis_size("win")
    stations, local_windows, _, samples = records.shape
    send_rows = send_table.reshape(-1)
    slots = send_rows.shape[0]
    chunks = samples // LANES
    pairs = observed.shape[0]
    combos = CHANS * CHANS
    share = pairs // window_groups
    corr_scale = 1.0 / math.sqrt(samples * local_windows * window_groups)
    adj_scale = 1.0 / math.sqrt(CHANS * LAGS)

    chips = slots // 2
    block = jax.ShapeDtypeStruct((CHANS, chunks, LANES), jnp.bfloat16)
    blocks = jax.ShapeDtypeStruct((chips, CHANS, chunks, LANES), jnp.bfloat16)
    any_space = pl.BlockSpec(memory_space=pltpu.HBM)
    planes = jnp.transpose(records, (1, 2, 0, 3)).reshape(CHANS, stations, samples)
    planes = pltpu.with_memory_space_constraint(planes, pltpu.HBM)
    send_rows, pair_first, pair_second, lag_lo, lag_hi = [
        pltpu.with_memory_space_constraint(x, pltpu.HBM)
        for x in (send_rows, pair_first, pair_second, lag_lo, lag_hi)
    ]
    swap, *keep = pl.pallas_call(
        pack_kernel,
        in_specs=[any_space, any_space],
        out_specs=[vmem()] * (1 + chips),
        out_shape=[blocks] + [block] * chips,
        scratch_shapes=[
            pltpu.VMEM((CHANS, stations, samples), jnp.bfloat16),
            pltpu.VMEM((CHANS, chunks * stations, LANES), jnp.float32),
            pltpu.SMEM((slots,), jnp.int32),
            pltpu.SemaphoreType.DMA((CHANS + 1,)),
        ],
        compiler_params=pltpu.CompilerParams(vmem_limit_bytes=8 * 2**20),
        name="pack",
    )(send_rows, planes)
    rows = 3 * LANES - HALF_TILE
    early = pairs * EARLY // 16
    fan_shape = jax.ShapeDtypeStruct((slots * CHANS, rows, LANES), jnp.bfloat16)
    corr_shape = jax.ShapeDtypeStruct((combos, early, LAGS), jnp.float32)
    late_shape = jax.ShapeDtypeStruct((combos, pairs - early, LAGS), jnp.float32)
    index_shape = jax.ShapeDtypeStruct((pairs,), jnp.int32)
    height = slots * CHANS * PHASES
    bands_shape = jax.ShapeDtypeStruct((slots, height, DEPTH), jnp.bfloat16)
    index_scratch = pltpu.SMEM((pairs,), jnp.int32)
    small = pltpu.CompilerParams(vmem_limit_bytes=16 * 2**20)
    cost = pl.CostEstimate(flops=2 * 10**9, bytes_accessed=2**22, transcendentals=0)
    seen = jnp.transpose(observed, (1, 2, 0, 3)).reshape(combos, pairs, LAGS)
    seen = pltpu.with_memory_space_constraint(seen, pltpu.HBM)
    bands, firsts, seconds, rows_copy, inside, seen, seen_later = pl.pallas_call(
        prep_kernel,
        in_specs=[pl.BlockSpec(memory_space=pl.ANY)] + [any_space] * 6,
        out_specs=[vmem()] * 7,
        out_shape=[
            bands_shape,
            index_shape,
            index_shape,
            jax.ShapeDtypeStruct((slots,), jnp.int32),
            jax.ShapeDtypeStruct((pairs, LAGS), jnp.int32),
            corr_shape,
            late_shape,
        ],
        scratch_shapes=[
            pltpu.VMEM((combos, pairs, LAGS), jnp.float32),
            index_scratch,
            index_scratch,
            pltpu.SemaphoreType.DMA((6,)),
        ],
        compiler_params=small,
        cost_estimate=cost,
        name="prep",
    )(swap, pair_first, pair_second, send_rows, lag_lo, lag_hi, seen)
    order, arrived = across(swap, keep, 1, lambda n: list(range(1,n)))

    corr, fan, heads = pl.pallas_call(
        functools.partial(corr_first_kernel, order),
        in_specs=[vmem()] * (chips + 3),
        out_specs=[vmem()] * 3,
        out_shape=[
            corr_shape,
            fan_shape,
            jax.ShapeDtypeStruct(
                (slots, CHANS * WIDE, HALF_TILE // WIDE * LANES), jnp.bfloat16
            ),
        ],
        scratch_shapes=[index_scratch, index_scratch, pltpu.SemaphoreType.DMA((2,))],
        compiler_params=small,
        cost_estimate=cost,
        name="corr_first",
    )(firsts, seconds, *arrived)
    parts = window_parts(corr)
    later = pl.pallas_call(
        functools.partial(corr_second_kernel, early),
        in_specs=[smem(), smem(), vmem(), vmem()],
        out_specs=vmem(),
        out_shape=late_shape,
        compiler_params=small,
        cost_estimate=cost,
        name="corr_second",
    )(firsts, seconds, fan, heads)
    later_parts = window_parts(later)

    lag_rows = pltpu.VMEM((combos, early, WINDOW), jnp.float32)
    bands, resid = pl.pallas_call(
        functools.partial(bands_kernel, corr_scale),
        in_specs=[vmem()] * (5 + len(parts)),
        out_specs=[vmem()] * 2,
        out_shape=[bands_shape, corr_shape],
        scratch_shapes=[
            lag_rows, lag_rows, index_scratch, index_scratch, pltpu.SemaphoreType.DMA((2,))
        ],
        input_output_aliases={4: 0},
        compiler_params=small,
        cost_estimate=cost,
        name="bands",
    )(firsts, seconds, inside, seen, bands, *parts)
    total = pltpu.VMEM((height // 2, 4 * LANES), jnp.float32)
    lag_rows = pltpu.VMEM((combos, pairs - early, WINDOW), jnp.float32)
    bands, swap, residual = pl.pallas_call(
        functools.partial(adjoint_kernel, corr_scale, adj_scale),
        in_specs=[vmem()] * (7 + len(later_parts)),
        out_specs=[vmem()] * 3,
        out_shape=[bands_shape, blocks, jax.ShapeDtypeStruct((combos, share, LAGS), jnp.float32)],
        scratch_shapes=[
            pltpu.VMEM((combos, pairs - early, LAGS), jnp.float32),
            lag_rows,
            lag_rows,
            total,
            index_scratch,
            index_scratch,
            pltpu.SemaphoreType.DMA((2,)),
        ],
        input_output_aliases={4: 0},
        compiler_params=small,
        cost_estimate=cost,
        name="adjoint",
    )(firsts, seconds, inside, seen_later, bands, fan, resid, *later_parts)
    keep = pl.pallas_call(
        functools.partial(keep_kernel, adj_scale),
        in_specs=[vmem()] * 2,
        out_specs=[vmem()] * chips,
        out_shape=[block] * chips,
        scratch_shapes=[total],
        compiler_params=small,
        cost_estimate=cost,
        name="keep",
    )(bands, fan)
    order, returned = across(swap, keep, -1, lambda n: list(range(n-1,0,-1)))
    stacked = pl.pallas_call(
        functools.partial(unpack_kernel, order),
        in_specs=[vmem()] * (chips + 2),
        out_specs=any_space,
        out_shape=jax.ShapeDtypeStruct((CHANS, stations, samples), jnp.bfloat16),
        scratch_shapes=[
            pltpu.VMEM((CHANS, stations, samples), jnp.bfloat16),
            pltpu.VMEM((CHANS, chunks * stations, LANES), jnp.float32),
            pltpu.SMEM((slots,), jnp.int32),
            pltpu.SemaphoreType.DMA((CHANS + 1,)),
        ],
        compiler_params=pltpu.CompilerParams(vmem_limit_bytes=8 * 2**20),
        name="unpack",
    )(rows_copy, *returned)
    station_adjoint = jnp.transpose(stacked.reshape(1, CHANS, stations, samples), (2, 0, 1, 3))
    residual = jnp.transpose(residual.reshape(CHANS, CHANS, share, LAGS), (2, 0, 1, 3))
    return (station_adjoint, residual)


def solution(mesh):
    placed = (
        P("stn", "win", None, None),
        P("stn", None, None, None),
        P("stn"),
        P("stn"),
        P("stn", None, None),
        P("stn"),
        P("stn"),
    )
    return jax.shard_map(
        shards,
        mesh=mesh,
        in_specs=placed,
        out_specs=(P("stn", "win", None, None), P(("stn", "win"), None, None, None)),
        check_vma=False,
    )
```

```python
import functools
import math

import jax
import jax.numpy as jnp
from jax import lax
from jax.experimental import pallas as pl
from jax.experimental.pallas import tpu as pltpu
from jax.sharding import PartitionSpec as P

LAGS = 256
HALF = LAGS // 2
LANES = 128
HALF_TILE = LANES // 2
PHASES = 16
WIDE = 32
EARLY = 14
CHANS = 3
WINDOW = 3 * LANES
DEPTH = 7 * LANES


def member(me, chips, step, other):
    return 2 * ((me // 2 + step) & (chips - 1)) + ((me & 1) ^ other)


def near_slot(q, me, chips):
    return 2 * ((me // 2 - q // 2) & (chips - 1)) + ((q ^ me) & 1)


def fetch(sources, targets, sems):
    copies = [pltpu.make_async_copy(s, t, sems.at[k]) for k, (s, t) in enumerate(zip(sources, targets))]
    for copy in copies:
        copy.start()
    return copies


def pack_kernel(rows_in, rec_ref, swap_ref, *refs):
    keep_refs = refs[:-4]
    buffer, scratch, rows_ref, sems = refs[-4:]
    me = lax.axis_index("stn")
    stations = rec_ref.shape[1]
    chunks = rec_ref.shape[2] // LANES
    copies = fetch(
        [rows_in] + [rec_ref.at[c] for c in range(CHANS)],
        [rows_ref] + [buffer.at[c] for c in range(CHANS)],
        sems,
    )
    copies[0].wait()
    for c in range(CHANS):
        copies[c + 1].wait()
        for r in range(chunks):
            piece = buffer[c, :, r * LANES:(r + 1) * LANES]
            scratch[c, r * stations:(r + 1) * stations, :] = piece.astype(jnp.float32)
        for j, keep_ref in enumerate(keep_refs):
            for i, ref in enumerate((keep_ref, swap_ref.at[j])):
                station = rows_ref[member(me, len(keep_refs), j, i)]
                picked = scratch[c, pl.ds(station, chunks, stride=stations), :]
                ref[c] = picked.astype(jnp.bfloat16)


def unpack_kernel(order, rows_in, *refs):
    returned = refs[:-5]
    out_ref, buffer, scratch, rows_ref, sems = refs[-5:]
    rows_copy = pltpu.make_async_copy(rows_in, rows_ref, sems.at[CHANS])
    rows_copy.start()
    scratch[...] = jnp.zeros_like(scratch)
    rows_copy.wait()
    me = lax.axis_index("stn")
    stations = out_ref.shape[1]
    chunks = out_ref.shape[2] // LANES
    copies = []
    for c in range(CHANS):
        pieces = [(2 * j + i, ref.at[i]) for j, ref in zip(order, returned[:-2]) for i in range(2)]
        for j, ref in pieces + [(0, returned[-2]), (1, returned[-1])]:
            station = rows_ref[member(me, len(order) - 1, j // 2, j % 2)]
            where = pl.ds(station, chunks, stride=stations)
            scratch[c, where, :] = scratch[c, where, :] + ref[c].astype(jnp.float32)
        for r in range(chunks):
            piece = scratch[c, r * stations:(r + 1) * stations, :]
            buffer[c, :, r * LANES:(r + 1) * LANES] = piece.astype(jnp.bfloat16)
        copies.append(pltpu.make_async_copy(buffer.at[c], out_ref.at[c], sems.at[c]))
        copies[c].start()
    for copy in copies:
        copy.wait()


def build_phases(slot_refs, fan_ref):
    chunks = slot_refs[0].shape[1]
    rows = fan_ref.shape[1]
    lane = lax.broadcasted_iota(jnp.int32, (LANES, LANES), 1)
    left = lax.broadcasted_iota(jnp.int32, (rows, LANES), 1) < chunks
    for place in range(0, CHANS * len(slot_refs), 2):
        pair = [slot_refs[e // CHANS][e % CHANS] for e in (place, place + 1)]
        middle = jnp.concatenate(pair, axis=0).astype(jnp.float32).T
        before = jnp.where(lane % chunks == 0, 0.0, pltpu.roll(middle, 1, 1))
        after = jnp.where(lane % chunks == chunks - 1, 0.0, pltpu.roll(middle, LANES - 1, 1))
        wide = jnp.concatenate([before, middle, after], axis=0)
        swapped = pltpu.roll(wide, chunks, 1)
        one = jnp.where(left, wide[:rows], swapped[HALF_TILE:])
        two = jnp.where(left, swapped[:rows], wide[HALF_TILE:])
        fan_ref[place] = one.astype(jnp.bfloat16)
        fan_ref[place + 1] = two.astype(jnp.bfloat16)


def shifted_rows(fan_ref, slot, phases):
    span = LAGS + phases
    tail = DEPTH - CHANS * span
    columns = []
    for first in range(0, HALF_TILE, phases):
        parts = [fan_ref[CHANS * slot + b, first:first + span, :] for b in range(CHANS)]
        parts.append(fan_ref[CHANS * slot, first:first + tail, :])
        columns.append(jnp.concatenate(parts, axis=0))
    return jnp.concatenate(columns, axis=1)


def prep_kernel(
    token, first_in, second_in, rows_in, low_in, high_in, observed_in,
    bands, first_out, second_out, rows_out, inside, seen, seen_later,
    staged, low_ref, high_ref, sems,
):
    copies = fetch(
        (low_in, high_in, observed_in, first_in, second_in, rows_in),
        (low_ref, high_ref, staged, first_out, second_out, rows_out),
        sems,
    )
    bands[...] = jnp.zeros_like(bands)
    for copy in copies:
        copy.wait()
    pairs = inside.shape[0]
    early = seen.shape[1]
    row = lax.broadcasted_iota(jnp.int32, (pairs, LAGS), 0)
    lag = lax.broadcasted_iota(jnp.int32, (pairs, LAGS), 1)
    low = jnp.zeros_like(row)
    high = jnp.zeros_like(row)
    for p in range(pairs):
        low = jnp.where(row == p, low_ref[p], low)
        high = jnp.where(row == p, high_ref[p], high)
    inside[...] = ((lag >= low) & (lag < high)).astype(jnp.int32)
    for i in range(seen.shape[0]):
        seen[i] = staged[i, :early]
        seen_later[i] = staged[i, early:]


def correlate(start, first_ref, second_ref, fan_ref, heads, corr_ref):
    me = lax.axis_index("stn")
    chips = heads.shape[0] // 2

    def step(p, carry):
        right = shifted_rows(fan_ref, near_slot(second_ref[start + p], me, chips), WIDE)
        products = lax.dot_general(
            heads[near_slot(first_ref[start + p], me, chips)], right, (((1,), (1,)), ((), ())),
            preferred_element_type=jnp.float32,
        )
        for a in range(CHANS):
            for b in range(CHANS):
                block = products[WIDE * a:WIDE * (a + 1), LAGS * b:LAGS * b + WINDOW]
                shift = WINDOW - WIDE * b - (WIDE - 1)
                turned = pltpu.roll(block, shift, 1, stride=1, stride_axis=0)
                corr_ref[CHANS * a + b, pl.ds(p, 1), :] = jnp.sum(
                    turned[:, :LAGS], axis=0, keepdims=True
                )
        return carry

    count = corr_ref.shape[1]
    lax.fori_loop(0, count, step, 0, unroll=min(count, 16))


def corr_first_kernel(order, first_in, second_in, *refs):
    given = refs[:-6]
    corr_ref, fan_ref, heads, first_ref, second_ref, sems = refs[-6:]
    copies = fetch((first_in, second_in), (first_ref, second_ref), sems)
    slot_refs = [None] * (2 * len(given) - 2)
    for j, ref in zip(order, given[:-2]):
        slot_refs[2 * j:2 * j + 2] = [ref.at[0], ref.at[1]]
    slot_refs[:2] = given[-2:]
    build_phases(slot_refs, fan_ref)
    height = CHANS * WIDE
    row = lax.broadcasted_iota(jnp.int32, (height, height), 0)
    column = lax.broadcasted_iota(jnp.int32, (height, height), 1)
    same = row // WIDE == column // WIDE
    flip = (same & (row % WIDE + column % WIDE == WIDE - 1)).astype(jnp.bfloat16)

    def head(q, carry):
        rows = []
        for a in range(CHANS):
            pieces = []
            for m in range(0, HALF_TILE, WIDE):
                pieces.append(fan_ref[CHANS * q + a, HALF + m:HALF + m + WIDE, :])
            rows.append(jnp.concatenate(pieces, axis=1))
        natural = jnp.concatenate(rows, axis=0)
        heads[q] = jnp.dot(flip, natural, preferred_element_type=jnp.float32).astype(jnp.bfloat16)
        return carry

    lax.fori_loop(0, heads.shape[0], head, 0, unroll=8)
    for copy in copies:
        copy.wait()
    correlate(0, first_ref, second_ref, fan_ref, heads, corr_ref)


def corr_second_kernel(start, first_ref, second_ref, fan_ref, heads, corr_ref):
    correlate(start, first_ref, second_ref, fan_ref, heads, corr_ref)


def spread(lag_rows, combos, p):
    turned = []
    for c, combo in enumerate(combos):
        block = jnp.broadcast_to(lag_rows[combo, pl.ds(p, 1), :], (PHASES, WINDOW))
        turned.append(pltpu.roll(block, PHASES * c, 1, stride=1, stride_axis=0))
    w0, w1, w2 = turned
    return jnp.concatenate(
        [
            w0[:, :LAGS],
            w0[:, LAGS:] + w1[:, :LANES],
            w1[:, LANES:LAGS],
            w1[:, LAGS:] + w2[:, :LANES],
            w2[:, LANES:],
        ],
        axis=1,
    ).astype(jnp.bfloat16)


def pairwise(terms):
    while len(terms) > 1:
        terms = [sum(terms[k + 1:k + 2], terms[k]) for k in range(0, len(terms), 2)]
    return terms[0]


def residuals(corr_scale, part_refs, observed_ref, inside, resid, forward, backward):
    combos, pairs, _ = resid.shape
    flip = (
        lax.broadcasted_iota(jnp.int32, (LAGS, WINDOW), 0)
        + lax.broadcasted_iota(jnp.int32, (LAGS, WINDOW), 1)
        == LAGS
    ).astype(jnp.bfloat16)
    forward[:, :, LAGS:] = jnp.zeros((combos, pairs, WINDOW - LAGS), jnp.float32)
    for i in range(combos):
        summed = pairwise([ref[i] for ref in part_refs])
        value = jnp.where(inside, summed * corr_scale - observed_ref[i], 0.0)
        resid[i] = value
        rounded = value.astype(jnp.bfloat16)
        forward[i, :, :LAGS] = rounded.astype(jnp.float32)
        backward[i] = jnp.dot(rounded, flip, preferred_element_type=jnp.float32)


def fill_bands(start, first_ref, second_ref, forward, backward, bands):
    me = lax.axis_index("stn")
    slots = bands.shape[0]
    pairs = forward.shape[1]
    height = CHANS * PHASES

    def row_place(q):
        return q // 2 + (slots // 2) * (1 - q % 2)

    def fill(p, carry):
        qf = near_slot(first_ref[start + p], me, slots // 2)
        qs = near_slot(second_ref[start + p], me, slots // 2)
        for c in range(CHANS):
            at = pl.multiple_of(height * row_place(qf) + PHASES * c, PHASES)
            bands[qs, pl.ds(at, PHASES), :] = spread(
                forward, [CHANS * c + b for b in range(CHANS)], p
            )
            at = pl.multiple_of(height * row_place(qs) + PHASES * c, PHASES)
            bands[qf, pl.ds(at, PHASES), :] = spread(
                backward, [CHANS * a + c for a in range(CHANS)], p
            )
        return carry

    lax.fori_loop(0, pairs, fill, 0, unroll=min(pairs, 16))


def contract(adj_scale, first_row, bands, fan_ref, total, outs):
    rows = total.shape[0]
    slots = bands.shape[0]
    group = 2
    for r in range(0, slots, group):
        right = jnp.concatenate(
            [shifted_rows(fan_ref, q, PHASES) for q in range(r, r + group)], axis=0
        )
        left = jnp.concatenate(
            [bands[q, first_row:first_row + rows, :] for q in range(r, r + group)], axis=1
        )
        product = jnp.dot(left, right, preferred_element_type=jnp.float32)
        total[...] = product if r == 0 else total[...] + product
    chunks = outs[0].shape[1]
    near = lax.broadcasted_iota(jnp.int32, (PHASES, LANES), 1) < chunks
    for place in range(0, rows // PHASES, 2):
        upper = []
        lower = []
        for m in range(4):
            columns = slice(m * LANES, (m + 1) * LANES)
            one = total[place * PHASES:(place + 1) * PHASES, columns]
            two = total[(place + 1) * PHASES:(place + 2) * PHASES, columns]
            upper.append(jnp.where(near, one, pltpu.roll(two, chunks, 1)))
            lower.append(jnp.where(near, pltpu.roll(one, chunks, 1), two))
        tile = (jnp.concatenate(upper + lower, axis=0).T * adj_scale).astype(jnp.bfloat16)
        for k in range(2):
            e = place + k
            outs[e // CHANS][e % CHANS] = tile[k * chunks:(k + 1) * chunks]


def bands_kernel(corr_scale, first_in, second_in, inside_ref, seen_ref, bands_in, *refs):
    part_refs = refs[:-7]
    bands, resid, forward, backward, first_ref, second_ref, sems = refs[-7:]
    copies = fetch((first_in, second_in), (first_ref, second_ref), sems)
    inside = inside_ref[:resid.shape[1], :] > 0
    residuals(corr_scale, part_refs, seen_ref, inside, resid, forward, backward)
    for copy in copies:
        copy.wait()
    fill_bands(0, first_ref, second_ref, forward, backward, bands)


def adjoint_kernel(
    corr_scale, adj_scale, first_in, second_in, inside_ref, seen_ref, bands_in, fan_ref,
    earlier, *refs
):
    (bands, swap_ref, share_ref, resid, forward, backward, total,
     first_ref, second_ref, sems) = refs[-10:]
    part_refs = refs[:-10]
    copies = fetch((first_in, second_in), (first_ref, second_ref), sems)
    half = earlier.shape[1]
    inside = inside_ref[half:, :] > 0
    residuals(corr_scale, part_refs, seen_ref, inside, resid, forward, backward)
    offset = lax.axis_index("win") * share_ref.shape[1]
    for j in range(share_ref.shape[1]):
        p = offset + j
        for i in range(resid.shape[0]):
            one = earlier[i, pl.ds(jnp.minimum(p, half - 1), 1), :]
            two = resid[i, pl.ds(jnp.maximum(p - half, 0), 1), :]
            share_ref[i, j:j + 1, :] = jnp.where(p < half, one, two)
    for copy in copies:
        copy.wait()
    fill_bands(half, first_ref, second_ref, forward, backward, bands)
    outs = [swap_ref.at[j] for j in range(swap_ref.shape[0])]
    contract(adj_scale, 0, bands, fan_ref, total, outs)


def keep_kernel(adj_scale, bands, fan_ref, *refs):
    outs = refs[:-1]
    total = refs[-1]
    contract(adj_scale, total.shape[0], bands, fan_ref, total, outs)


def smem():
    return pl.BlockSpec(memory_space=pltpu.SMEM)


def vmem():
    return pl.BlockSpec(memory_space=pltpu.VMEM)


def flipped(x, axis, bits):
    count = lax.axis_size(axis)
    return lax.ppermute(x, axis, [(k, k ^ bits) for k in range(count)])


def across(swap, keep, sign, first):
    chips = len(keep)
    got = flipped(swap, "stn", 1)
    order = first(chips)
    blocks = []
    for j in order:
        pairs = [(k, (k + 2 * sign * j) % (2 * chips)) for k in range(2 * chips)]
        blocks.append(lax.ppermute(jnp.stack([keep[j], got[j]]), "stn", pairs))
    return order + [0, 0], blocks + [keep[0], got[0]]


def window_parts(corr):
    groups = lax.axis_size("win")
    if groups > 4:
        gathered = lax.all_gather(corr, "win")
        return [gathered[w] for w in range(groups)]
    return [corr] + [flipped(corr, "win", w) for w in range(1, groups)]


def shards(records, observed, lag_lo, lag_hi, send_table, pair_first, pair_second):
    owner_count = lax.axis_size("stn")
    window_groups = lax.axis_size("win")
    stations, local_windows, _, samples = records.shape
    send_rows = send_table.reshape(-1)
    slots = send_rows.shape[0]
    chunks = samples // LANES
    pairs = observed.shape[0]
    combos = CHANS * CHANS
    share = pairs // window_groups
    corr_scale = 1.0 / math.sqrt(samples * local_windows * window_groups)
    adj_scale = 1.0 / math.sqrt(CHANS * LAGS)

    chips = slots // 2
    block = jax.ShapeDtypeStruct((CHANS, chunks, LANES), jnp.bfloat16)
    blocks = jax.ShapeDtypeStruct((chips, CHANS, chunks, LANES), jnp.bfloat16)
    any_space = pl.BlockSpec(memory_space=pltpu.HBM)
    planes = jnp.transpose(records, (1, 2, 0, 3)).reshape(CHANS, stations, samples)
    planes = pltpu.with_memory_space_constraint(planes, pltpu.HBM)
    send_rows, pair_first, pair_second, lag_lo, lag_hi = [
        pltpu.with_memory_space_constraint(x, pltpu.HBM)
        for x in (send_rows, pair_first, pair_second, lag_lo, lag_hi)
    ]
    swap, *keep = pl.pallas_call(
        pack_kernel,
        in_specs=[any_space, any_space],
        out_specs=[vmem()] * (1 + chips),
        out_shape=[blocks] + [block] * chips,
        scratch_shapes=[
            pltpu.VMEM((CHANS, stations, samples), jnp.bfloat16),
            pltpu.VMEM((CHANS, chunks * stations, LANES), jnp.float32),
            pltpu.SMEM((slots,), jnp.int32),
            pltpu.SemaphoreType.DMA((CHANS + 1,)),
        ],
        compiler_params=pltpu.CompilerParams(vmem_limit_bytes=8 * 2**20),
        name="pack",
    )(send_rows, planes)
    rows = 3 * LANES - HALF_TILE
    early = pairs * EARLY // 16
    fan_shape = jax.ShapeDtypeStruct((slots * CHANS, rows, LANES), jnp.bfloat16)
    corr_shape = jax.ShapeDtypeStruct((combos, early, LAGS), jnp.float32)
    late_shape = jax.ShapeDtypeStruct((combos, pairs - early, LAGS), jnp.float32)
    index_shape = jax.ShapeDtypeStruct((pairs,), jnp.int32)
    height = slots * CHANS * PHASES
    bands_shape = jax.ShapeDtypeStruct((slots, height, DEPTH), jnp.bfloat16)
    index_scratch = pltpu.SMEM((pairs,), jnp.int32)
    small = pltpu.CompilerParams(vmem_limit_bytes=16 * 2**20)
    cost = pl.CostEstimate(flops=2 * 10**9, bytes_accessed=2**22, transcendentals=0)
    seen = jnp.transpose(observed, (1, 2, 0, 3)).reshape(combos, pairs, LAGS)
    seen = pltpu.with_memory_space_constraint(seen, pltpu.HBM)
    bands, firsts, seconds, rows_copy, inside, seen, seen_later = pl.pallas_call(
        prep_kernel,
        in_specs=[pl.BlockSpec(memory_space=pl.ANY)] + [any_space] * 6,
        out_specs=[vmem()] * 7,
        out_shape=[
            bands_shape,
            index_shape,
            index_shape,
            jax.ShapeDtypeStruct((slots,), jnp.int32),
            jax.ShapeDtypeStruct((pairs, LAGS), jnp.int32),
            corr_shape,
            late_shape,
        ],
        scratch_shapes=[
            pltpu.VMEM((combos, pairs, LAGS), jnp.float32),
            index_scratch,
            index_scratch,
            pltpu.SemaphoreType.DMA((6,)),
        ],
        compiler_params=small,
        cost_estimate=cost,
        name="prep",
    )(swap, pair_first, pair_second, send_rows, lag_lo, lag_hi, seen)
    order, arrived = across(swap, keep, 1, lambda n: list(range(1,n)))

    corr, fan, heads = pl.pallas_call(
        functools.partial(corr_first_kernel, order),
        in_specs=[vmem()] * (chips + 3),
        out_specs=[vmem()] * 3,
        out_shape=[
            corr_shape,
            fan_shape,
            jax.ShapeDtypeStruct(
                (slots, CHANS * WIDE, HALF_TILE // WIDE * LANES), jnp.bfloat16
            ),
        ],
        scratch_shapes=[index_scratch, index_scratch, pltpu.SemaphoreType.DMA((2,))],
        compiler_params=small,
        cost_estimate=cost,
        name="corr_first",
    )(firsts, seconds, *arrived)
    parts = window_parts(corr)
    later = pl.pallas_call(
        functools.partial(corr_second_kernel, early),
        in_specs=[smem(), smem(), vmem(), vmem()],
        out_specs=vmem(),
        out_shape=late_shape,
        compiler_params=small,
        cost_estimate=cost,
        name="corr_second",
    )(firsts, seconds, fan, heads)
    later_parts = window_parts(later)

    lag_rows = pltpu.VMEM((combos, early, WINDOW), jnp.float32)
    bands, resid = pl.pallas_call(
        functools.partial(bands_kernel, corr_scale),
        in_specs=[vmem()] * (5 + len(parts)),
        out_specs=[vmem()] * 2,
        out_shape=[bands_shape, corr_shape],
        scratch_shapes=[
            lag_rows, lag_rows, index_scratch, index_scratch, pltpu.SemaphoreType.DMA((2,))
        ],
        input_output_aliases={4: 0},
        compiler_params=small,
        cost_estimate=cost,
        name="bands",
    )(firsts, seconds, inside, seen, bands, *parts)
    total = pltpu.VMEM((height // 2, 4 * LANES), jnp.float32)
    lag_rows = pltpu.VMEM((combos, pairs - early, WINDOW), jnp.float32)
    bands, swap, residual = pl.pallas_call(
        functools.partial(adjoint_kernel, corr_scale, adj_scale),
        in_specs=[vmem()] * (7 + len(later_parts)),
        out_specs=[vmem()] * 3,
        out_shape=[bands_shape, blocks, jax.ShapeDtypeStruct((combos, share, LAGS), jnp.float32)],
        scratch_shapes=[
            pltpu.VMEM((combos, pairs - early, LAGS), jnp.float32),
            lag_rows,
            lag_rows,
            total,
            index_scratch,
            index_scratch,
            pltpu.SemaphoreType.DMA((2,)),
        ],
        input_output_aliases={4: 0},
        compiler_params=small,
        cost_estimate=cost,
        name="adjoint",
    )(firsts, seconds, inside, seen_later, bands, fan, resid, *later_parts)
    keep = pl.pallas_call(
        functools.partial(keep_kernel, adj_scale),
        in_specs=[vmem()] * 2,
        out_specs=[vmem()] * chips,
        out_shape=[block] * chips,
        scratch_shapes=[total],
        compiler_params=small,
        cost_estimate=cost,
        name="keep",
    )(bands, fan)
    order, returned = across(swap, keep, -1, lambda n: list(range(n-1,0,-1)))
    stacked = pl.pallas_call(
        functools.partial(unpack_kernel, order),
        in_specs=[vmem()] * (chips + 2),
        out_specs=any_space,
        out_shape=jax.ShapeDtypeStruct((CHANS, stations, samples), jnp.bfloat16),
        scratch_shapes=[
            pltpu.VMEM((CHANS, stations, samples), jnp.bfloat16),
            pltpu.VMEM((CHANS, chunks * stations, LANES), jnp.float32),
            pltpu.SMEM((slots,), jnp.int32),
            pltpu.SemaphoreType.DMA((CHANS + 1,)),
        ],
        compiler_params=pltpu.CompilerParams(vmem_limit_bytes=8 * 2**20),
        name="unpack",
    )(rows_copy, *returned)
    station_adjoint = jnp.transpose(stacked.reshape(1, CHANS, stations, samples), (2, 0, 1, 3))
    residual = jnp.transpose(residual.reshape(CHANS, CHANS, share, LAGS), (2, 0, 1, 3))
    return (station_adjoint, residual)


def solution(mesh):
    placed = (
        P("stn", "win", None, None),
        P("stn", None, None, None),
        P("stn"),
        P("stn"),
        P("stn", None, None),
        P("stn"),
        P("stn"),
    )
    return jax.shard_map(
        shards,
        mesh=mesh,
        in_specs=placed,
        out_specs=(P("stn", "win", None, None), P(("stn", "win"), None, None, None)),
        check_vma=False,
    )
```

```python
import functools
import math

import jax
import jax.numpy as jnp
from jax import lax
from jax.experimental import pallas as pl
from jax.experimental.pallas import tpu as pltpu
from jax.sharding import PartitionSpec as P

LAGS = 256
HALF = LAGS // 2
LANES = 128
HALF_TILE = LANES // 2
PHASES = 16
WIDE = 32
EARLY = 14
CHANS = 3
WINDOW = 3 * LANES
DEPTH = 7 * LANES


def member(me, chips, step, other):
    return 2 * ((me // 2 + step) & (chips - 1)) + ((me & 1) ^ other)


def near_slot(q, me, chips):
    return 2 * ((me // 2 - q // 2) & (chips - 1)) + ((q ^ me) & 1)


def fetch(sources, targets, sems):
    copies = [pltpu.make_async_copy(s, t, sems.at[k]) for k, (s, t) in enumerate(zip(sources, targets))]
    for copy in copies:
        copy.start()
    return copies


def pack_kernel(rows_in, rec_ref, swap_ref, *refs):
    keep_refs = refs[:-4]
    buffer, scratch, rows_ref, sems = refs[-4:]
    me = lax.axis_index("stn")
    stations = rec_ref.shape[1]
    chunks = rec_ref.shape[2] // LANES
    copies = fetch(
        [rows_in] + [rec_ref.at[c] for c in range(CHANS)],
        [rows_ref] + [buffer.at[c] for c in range(CHANS)],
        sems,
    )
    copies[0].wait()
    for c in range(CHANS):
        copies[c + 1].wait()
        for r in range(chunks):
            piece = buffer[c, :, r * LANES:(r + 1) * LANES]
            scratch[c, r * stations:(r + 1) * stations, :] = piece.astype(jnp.float32)
        for j, keep_ref in enumerate(keep_refs):
            for i, ref in enumerate((keep_ref, swap_ref.at[j])):
                station = rows_ref[member(me, len(keep_refs), j, i)]
                picked = scratch[c, pl.ds(station, chunks, stride=stations), :]
                ref[c] = picked.astype(jnp.bfloat16)


def unpack_kernel(order, rows_in, *refs):
    returned = refs[:-5]
    out_ref, buffer, scratch, rows_ref, sems = refs[-5:]
    rows_copy = pltpu.make_async_copy(rows_in, rows_ref, sems.at[CHANS])
    rows_copy.start()
    scratch[...] = jnp.zeros_like(scratch)
    rows_copy.wait()
    me = lax.axis_index("stn")
    stations = out_ref.shape[1]
    chunks = out_ref.shape[2] // LANES
    copies = []
    for c in range(CHANS):
        pieces = [(2 * j + i, ref.at[i]) for j, ref in zip(order, returned[:-2]) for i in range(2)]
        for j, ref in pieces + [(0, returned[-2]), (1, returned[-1])]:
            station = rows_ref[member(me, len(order) - 1, j // 2, j % 2)]
            where = pl.ds(station, chunks, stride=stations)
            scratch[c, where, :] = scratch[c, where, :] + ref[c].astype(jnp.float32)
        for r in range(chunks):
            piece = scratch[c, r * stations:(r + 1) * stations, :]
            buffer[c, :, r * LANES:(r + 1) * LANES] = piece.astype(jnp.bfloat16)
        copies.append(pltpu.make_async_copy(buffer.at[c], out_ref.at[c], sems.at[c]))
        copies[c].start()
    for copy in copies:
        copy.wait()


def build_phases(slot_refs, fan_ref, first_slot):
    chunks = slot_refs[0].shape[1]
    rows = fan_ref.shape[1]
    lane = lax.broadcasted_iota(jnp.int32, (LANES, LANES), 1)
    left = lax.broadcasted_iota(jnp.int32, (rows, LANES), 1) < chunks
    for place in range(0, CHANS * len(slot_refs), 2):
        pair = [slot_refs[e // CHANS][e % CHANS] for e in (place, place + 1)]
        middle = jnp.concatenate(pair, axis=0).astype(jnp.float32).T
        before = jnp.where(lane % chunks == 0, 0.0, pltpu.roll(middle, 1, 1))
        after = jnp.where(lane % chunks == chunks - 1, 0.0, pltpu.roll(middle, LANES - 1, 1))
        wide = jnp.concatenate([before, middle, after], axis=0)
        swapped = pltpu.roll(wide, chunks, 1)
        one = jnp.where(left, wide[:rows], swapped[HALF_TILE:])
        two = jnp.where(left, swapped[:rows], wide[HALF_TILE:])
        fan_ref[CHANS * first_slot + place] = one.astype(jnp.bfloat16)
        fan_ref[CHANS * first_slot + place + 1] = two.astype(jnp.bfloat16)


def shifted_rows(fan_ref, slot, phases):
    span = LAGS + phases
    tail = DEPTH - CHANS * span
    columns = []
    for first in range(0, HALF_TILE, phases):
        parts = [fan_ref[CHANS * slot + b, first:first + span, :] for b in range(CHANS)]
        parts.append(fan_ref[CHANS * slot, first:first + tail, :])
        columns.append(jnp.concatenate(parts, axis=0))
    return jnp.concatenate(columns, axis=1)


def prep_kernel(
    own_ref, got_ref, first_in, second_in, rows_in, low_in, high_in, observed_in,
    bands, fan_ref, first_out, second_out, rows_out, inside, seen, seen_later,
    staged, low_ref, high_ref, sems,
):
    copies = fetch(
        (low_in, high_in, observed_in, first_in, second_in, rows_in),
        (low_ref, high_ref, staged, first_out, second_out, rows_out),
        sems,
    )
    bands[...] = jnp.zeros_like(bands)
    build_phases([own_ref, got_ref], fan_ref, 0)
    for copy in copies:
        copy.wait()
    pairs = inside.shape[0]
    early = seen.shape[1]
    row = lax.broadcasted_iota(jnp.int32, (pairs, LAGS), 0)
    lag = lax.broadcasted_iota(jnp.int32, (pairs, LAGS), 1)
    low = jnp.zeros_like(row)
    high = jnp.zeros_like(row)
    for p in range(pairs):
        low = jnp.where(row == p, low_ref[p], low)
        high = jnp.where(row == p, high_ref[p], high)
    inside[...] = ((lag >= low) & (lag < high)).astype(jnp.int32)
    for i in range(seen.shape[0]):
        seen[i] = staged[i, :early]
        seen_later[i] = staged[i, early:]


def correlate(start, first_ref, second_ref, fan_ref, heads, corr_ref):
    me = lax.axis_index("stn")
    chips = heads.shape[0] // 2

    def step(p, carry):
        right = shifted_rows(fan_ref, near_slot(second_ref[start + p], me, chips), WIDE)
        products = lax.dot_general(
            heads[near_slot(first_ref[start + p], me, chips)], right, (((1,), (1,)), ((), ())),
            preferred_element_type=jnp.float32,
        )
        for a in range(CHANS):
            for b in range(CHANS):
                block = products[WIDE * a:WIDE * (a + 1), LAGS * b:LAGS * b + WINDOW]
                shift = WINDOW - WIDE * b - (WIDE - 1)
                turned = pltpu.roll(block, shift, 1, stride=1, stride_axis=0)
                corr_ref[CHANS * a + b, pl.ds(p, 1), :] = jnp.sum(
                    turned[:, :LAGS], axis=0, keepdims=True
                )
        return carry

    count = corr_ref.shape[1]
    lax.fori_loop(0, count, step, 0, unroll=min(count, 16))


def corr_first_kernel(order, first_in, second_in, fan_in, *refs):
    given = refs[:-6]
    corr_ref, fan_ref, heads, first_ref, second_ref, sems = refs[-6:]
    copies = fetch((first_in, second_in), (first_ref, second_ref), sems)
    slot_refs = [None] * (2 * len(given))
    for j, ref in zip(order, given):
        slot_refs[2 * j - 2:2 * j] = [ref.at[0], ref.at[1]]
    build_phases(slot_refs, fan_ref, 2)
    height = CHANS * WIDE
    row = lax.broadcasted_iota(jnp.int32, (height, height), 0)
    column = lax.broadcasted_iota(jnp.int32, (height, height), 1)
    same = row // WIDE == column // WIDE
    flip = (same & (row % WIDE + column % WIDE == WIDE - 1)).astype(jnp.bfloat16)

    def head(q, carry):
        rows = []
        for a in range(CHANS):
            pieces = []
            for m in range(0, HALF_TILE, WIDE):
                pieces.append(fan_ref[CHANS * q + a, HALF + m:HALF + m + WIDE, :])
            rows.append(jnp.concatenate(pieces, axis=1))
        natural = jnp.concatenate(rows, axis=0)
        heads[q] = jnp.dot(flip, natural, preferred_element_type=jnp.float32).astype(jnp.bfloat16)
        return carry

    lax.fori_loop(0, heads.shape[0], head, 0, unroll=8)
    for copy in copies:
        copy.wait()
    correlate(0, first_ref, second_ref, fan_ref, heads, corr_ref)


def corr_second_kernel(start, first_ref, second_ref, fan_ref, heads, corr_ref):
    correlate(start, first_ref, second_ref, fan_ref, heads, corr_ref)


def spread(lag_rows, combos, p):
    turned = []
    for c, combo in enumerate(combos):
        block = jnp.broadcast_to(lag_rows[combo, pl.ds(p, 1), :], (PHASES, WINDOW))
        turned.append(pltpu.roll(block, PHASES * c, 1, stride=1, stride_axis=0))
    w0, w1, w2 = turned
    return jnp.concatenate(
        [
            w0[:, :LAGS],
            w0[:, LAGS:] + w1[:, :LANES],
            w1[:, LANES:LAGS],
            w1[:, LAGS:] + w2[:, :LANES],
            w2[:, LANES:],
        ],
        axis=1,
    ).astype(jnp.bfloat16)


def pairwise(terms):
    while len(terms) > 1:
        terms = [sum(terms[k + 1:k + 2], terms[k]) for k in range(0, len(terms), 2)]
    return terms[0]


def residuals(corr_scale, part_refs, observed_ref, inside, resid, forward, backward):
    combos, pairs, _ = resid.shape
    flip = (
        lax.broadcasted_iota(jnp.int32, (LAGS, WINDOW), 0)
        + lax.broadcasted_iota(jnp.int32, (LAGS, WINDOW), 1)
        == LAGS
    ).astype(jnp.bfloat16)
    forward[:, :, LAGS:] = jnp.zeros((combos, pairs, WINDOW - LAGS), jnp.float32)
    for i in range(combos):
        summed = pairwise([ref[i] for ref in part_refs])
        value = jnp.where(inside, summed * corr_scale - observed_ref[i], 0.0)
        resid[i] = value
        rounded = value.astype(jnp.bfloat16)
        forward[i, :, :LAGS] = rounded.astype(jnp.float32)
        backward[i] = jnp.dot(rounded, flip, preferred_element_type=jnp.float32)


def fill_bands(start, first_ref, second_ref, forward, backward, bands):
    me = lax.axis_index("stn")
    slots = bands.shape[0]
    pairs = forward.shape[1]
    height = CHANS * PHASES

    def row_place(q):
        return q // 2 + (slots // 2) * (1 - q % 2)

    def fill(p, carry):
        qf = near_slot(first_ref[start + p], me, slots // 2)
        qs = near_slot(second_ref[start + p], me, slots // 2)
        for c in range(CHANS):
            at = pl.multiple_of(height * row_place(qf) + PHASES * c, PHASES)
            bands[qs, pl.ds(at, PHASES), :] = spread(
                forward, [CHANS * c + b for b in range(CHANS)], p
            )
            at = pl.multiple_of(height * row_place(qs) + PHASES * c, PHASES)
            bands[qf, pl.ds(at, PHASES), :] = spread(
                backward, [CHANS * a + c for a in range(CHANS)], p
            )
        return carry

    lax.fori_loop(0, pairs, fill, 0, unroll=min(pairs, 16))


def contract(adj_scale, first_row, bands, fan_ref, total, outs):
    rows = total.shape[0]
    slots = bands.shape[0]
    group = 2
    for r in range(0, slots, group):
        right = jnp.concatenate(
            [shifted_rows(fan_ref, q, PHASES) for q in range(r, r + group)], axis=0
        )
        left = jnp.concatenate(
            [bands[q, first_row:first_row + rows, :] for q in range(r, r + group)], axis=1
        )
        product = jnp.dot(left, right, preferred_element_type=jnp.float32)
        total[...] = product if r == 0 else total[...] + product
    chunks = outs[0].shape[1]
    near = lax.broadcasted_iota(jnp.int32, (PHASES, LANES), 1) < chunks
    for place in range(0, rows // PHASES, 2):
        upper = []
        lower = []
        for m in range(4):
            columns = slice(m * LANES, (m + 1) * LANES)
            one = total[place * PHASES:(place + 1) * PHASES, columns]
            two = total[(place + 1) * PHASES:(place + 2) * PHASES, columns]
            upper.append(jnp.where(near, one, pltpu.roll(two, chunks, 1)))
            lower.append(jnp.where(near, pltpu.roll(one, chunks, 1), two))
        tile = (jnp.concatenate(upper + lower, axis=0).T * adj_scale).astype(jnp.bfloat16)
        for k in range(2):
            e = place + k
            outs[e // CHANS][e % CHANS] = tile[k * chunks:(k + 1) * chunks]


def bands_kernel(corr_scale, first_in, second_in, inside_ref, seen_ref, bands_in, *refs):
    part_refs = refs[:-7]
    bands, resid, forward, backward, first_ref, second_ref, sems = refs[-7:]
    copies = fetch((first_in, second_in), (first_ref, second_ref), sems)
    inside = inside_ref[:resid.shape[1], :] > 0
    residuals(corr_scale, part_refs, seen_ref, inside, resid, forward, backward)
    for copy in copies:
        copy.wait()
    fill_bands(0, first_ref, second_ref, forward, backward, bands)


def adjoint_kernel(
    corr_scale, adj_scale, first_in, second_in, inside_ref, seen_ref, bands_in, fan_ref,
    earlier, *refs
):
    (bands, swap_ref, share_ref, resid, forward, backward, total,
     first_ref, second_ref, sems) = refs[-10:]
    part_refs = refs[:-10]
    copies = fetch((first_in, second_in), (first_ref, second_ref), sems)
    half = earlier.shape[1]
    inside = inside_ref[half:, :] > 0
    residuals(corr_scale, part_refs, seen_ref, inside, resid, forward, backward)
    offset = lax.axis_index("win") * share_ref.shape[1]
    for j in range(share_ref.shape[1]):
        p = offset + j
        for i in range(resid.shape[0]):
            one = earlier[i, pl.ds(jnp.minimum(p, half - 1), 1), :]
            two = resid[i, pl.ds(jnp.maximum(p - half, 0), 1), :]
            share_ref[i, j:j + 1, :] = jnp.where(p < half, one, two)
    for copy in copies:
        copy.wait()
    fill_bands(half, first_ref, second_ref, forward, backward, bands)
    outs = [swap_ref.at[j] for j in range(swap_ref.shape[0])]
    contract(adj_scale, 0, bands, fan_ref, total, outs)


def keep_kernel(adj_scale, bands, fan_ref, *refs):
    outs = refs[:-1]
    total = refs[-1]
    contract(adj_scale, total.shape[0], bands, fan_ref, total, outs)


def smem():
    return pl.BlockSpec(memory_space=pltpu.SMEM)


def vmem():
    return pl.BlockSpec(memory_space=pltpu.VMEM)


def flipped(x, axis, bits):
    count = lax.axis_size(axis)
    return lax.ppermute(x, axis, [(k, k ^ bits) for k in range(count)])


def across(swap, keep, sign, first):
    chips = len(keep)
    got = flipped(swap, "stn", 1)
    order = first(chips)
    blocks = []
    for j in order:
        pairs = [(k, (k + 2 * sign * j) % (2 * chips)) for k in range(2 * chips)]
        blocks.append(lax.ppermute(jnp.stack([keep[j], got[j]]), "stn", pairs))
    return order + [0, 0], blocks + [keep[0], got[0]]


def window_parts(corr):
    groups = lax.axis_size("win")
    if groups > 4:
        gathered = lax.all_gather(corr, "win")
        return [gathered[w] for w in range(groups)]
    return [corr] + [flipped(corr, "win", w) for w in range(1, groups)]


def shards(records, observed, lag_lo, lag_hi, send_table, pair_first, pair_second):
    owner_count = lax.axis_size("stn")
    window_groups = lax.axis_size("win")
    stations, local_windows, _, samples = records.shape
    send_rows = send_table.reshape(-1)
    slots = send_rows.shape[0]
    chunks = samples // LANES
    pairs = observed.shape[0]
    combos = CHANS * CHANS
    share = pairs // window_groups
    corr_scale = 1.0 / math.sqrt(samples * local_windows * window_groups)
    adj_scale = 1.0 / math.sqrt(CHANS * LAGS)

    chips = slots // 2
    block = jax.ShapeDtypeStruct((CHANS, chunks, LANES), jnp.bfloat16)
    blocks = jax.ShapeDtypeStruct((chips, CHANS, chunks, LANES), jnp.bfloat16)
    any_space = pl.BlockSpec(memory_space=pltpu.HBM)
    planes = jnp.transpose(records, (1, 2, 0, 3)).reshape(CHANS, stations, samples)
    planes = pltpu.with_memory_space_constraint(planes, pltpu.HBM)
    send_rows, pair_first, pair_second, lag_lo, lag_hi = [
        pltpu.with_memory_space_constraint(x, pltpu.HBM)
        for x in (send_rows, pair_first, pair_second, lag_lo, lag_hi)
    ]
    swap, *keep = pl.pallas_call(
        pack_kernel,
        in_specs=[any_space, any_space],
        out_specs=[vmem()] * (1 + chips),
        out_shape=[blocks] + [block] * chips,
        scratch_shapes=[
            pltpu.VMEM((CHANS, stations, samples), jnp.bfloat16),
            pltpu.VMEM((CHANS, chunks * stations, LANES), jnp.float32),
            pltpu.SMEM((slots,), jnp.int32),
            pltpu.SemaphoreType.DMA((CHANS + 1,)),
        ],
        compiler_params=pltpu.CompilerParams(vmem_limit_bytes=8 * 2**20),
        name="pack",
    )(send_rows, planes)
    rows = 3 * LANES - HALF_TILE
    early = pairs * EARLY // 16
    fan_shape = jax.ShapeDtypeStruct((slots * CHANS, rows, LANES), jnp.bfloat16)
    corr_shape = jax.ShapeDtypeStruct((combos, early, LAGS), jnp.float32)
    late_shape = jax.ShapeDtypeStruct((combos, pairs - early, LAGS), jnp.float32)
    index_shape = jax.ShapeDtypeStruct((pairs,), jnp.int32)
    height = slots * CHANS * PHASES
    bands_shape = jax.ShapeDtypeStruct((slots, height, DEPTH), jnp.bfloat16)
    index_scratch = pltpu.SMEM((pairs,), jnp.int32)
    small = pltpu.CompilerParams(vmem_limit_bytes=16 * 2**20)
    cost = pl.CostEstimate(flops=2 * 10**9, bytes_accessed=2**22, transcendentals=0)
    seen = jnp.transpose(observed, (1, 2, 0, 3)).reshape(combos, pairs, LAGS)
    seen = pltpu.with_memory_space_constraint(seen, pltpu.HBM)
    order, arrived = across(swap, keep, 1, lambda n: list(range(1,n)))
    bands, fan, firsts, seconds, rows_copy, inside, seen, seen_later = pl.pallas_call(
        prep_kernel,
        in_specs=[vmem()] * 2 + [any_space] * 6,
        out_specs=[vmem()] * 8,
        out_shape=[
            bands_shape,
            fan_shape,
            index_shape,
            index_shape,
            jax.ShapeDtypeStruct((slots,), jnp.int32),
            jax.ShapeDtypeStruct((pairs, LAGS), jnp.int32),
            corr_shape,
            late_shape,
        ],
        scratch_shapes=[
            pltpu.VMEM((combos, pairs, LAGS), jnp.float32),
            index_scratch,
            index_scratch,
            pltpu.SemaphoreType.DMA((6,)),
        ],
        compiler_params=small,
        cost_estimate=cost,
        name="prep",
    )(*arrived[-2:], pair_first, pair_second, send_rows, lag_lo, lag_hi, seen)

    corr, fan, heads = pl.pallas_call(
        functools.partial(corr_first_kernel, order),
        in_specs=[vmem()] * (chips + 2),
        out_specs=[vmem()] * 3,
        out_shape=[
            corr_shape,
            fan_shape,
            jax.ShapeDtypeStruct(
                (slots, CHANS * WIDE, HALF_TILE // WIDE * LANES), jnp.bfloat16
            ),
        ],
        scratch_shapes=[index_scratch, index_scratch, pltpu.SemaphoreType.DMA((2,))],
        input_output_aliases={2: 1},
        compiler_params=small,
        cost_estimate=cost,
        name="corr_first",
    )(firsts, seconds, fan, *arrived[:-2])
    parts = window_parts(corr)
    later = pl.pallas_call(
        functools.partial(corr_second_kernel, early),
        in_specs=[smem(), smem(), vmem(), vmem()],
        out_specs=vmem(),
        out_shape=late_shape,
        compiler_params=small,
        cost_estimate=cost,
        name="corr_second",
    )(firsts, seconds, fan, heads)
    later_parts = window_parts(later)

    lag_rows = pltpu.VMEM((combos, early, WINDOW), jnp.float32)
    bands, resid = pl.pallas_call(
        functools.partial(bands_kernel, corr_scale),
        in_specs=[vmem()] * (5 + len(parts)),
        out_specs=[vmem()] * 2,
        out_shape=[bands_shape, corr_shape],
        scratch_shapes=[
            lag_rows, lag_rows, index_scratch, index_scratch, pltpu.SemaphoreType.DMA((2,))
        ],
        input_output_aliases={4: 0},
        compiler_params=small,
        cost_estimate=cost,
        name="bands",
    )(firsts, seconds, inside, seen, bands, *parts)
    total = pltpu.VMEM((height // 2, 4 * LANES), jnp.float32)
    lag_rows = pltpu.VMEM((combos, pairs - early, WINDOW), jnp.float32)
    bands, swap, residual = pl.pallas_call(
        functools.partial(adjoint_kernel, corr_scale, adj_scale),
        in_specs=[vmem()] * (7 + len(later_parts)),
        out_specs=[vmem()] * 3,
        out_shape=[bands_shape, blocks, jax.ShapeDtypeStruct((combos, share, LAGS), jnp.float32)],
        scratch_shapes=[
            pltpu.VMEM((combos, pairs - early, LAGS), jnp.float32),
            lag_rows,
            lag_rows,
            total,
            index_scratch,
            index_scratch,
            pltpu.SemaphoreType.DMA((2,)),
        ],
        input_output_aliases={4: 0},
        compiler_params=small,
        cost_estimate=cost,
        name="adjoint",
    )(firsts, seconds, inside, seen_later, bands, fan, resid, *later_parts)
    keep = pl.pallas_call(
        functools.partial(keep_kernel, adj_scale),
        in_specs=[vmem()] * 2,
        out_specs=[vmem()] * chips,
        out_shape=[block] * chips,
        scratch_shapes=[total],
        compiler_params=small,
        cost_estimate=cost,
        name="keep",
    )(bands, fan)
    order, returned = across(swap, keep, -1, lambda n: list(range(n-1,0,-1)))
    stacked = pl.pallas_call(
        functools.partial(unpack_kernel, order),
        in_specs=[vmem()] * (chips + 2),
        out_specs=any_space,
        out_shape=jax.ShapeDtypeStruct((CHANS, stations, samples), jnp.bfloat16),
        scratch_shapes=[
            pltpu.VMEM((CHANS, stations, samples), jnp.bfloat16),
            pltpu.VMEM((CHANS, chunks * stations, LANES), jnp.float32),
            pltpu.SMEM((slots,), jnp.int32),
            pltpu.SemaphoreType.DMA((CHANS + 1,)),
        ],
        compiler_params=pltpu.CompilerParams(vmem_limit_bytes=8 * 2**20),
        name="unpack",
    )(rows_copy, *returned)
    station_adjoint = jnp.transpose(stacked.reshape(1, CHANS, stations, samples), (2, 0, 1, 3))
    residual = jnp.transpose(residual.reshape(CHANS, CHANS, share, LAGS), (2, 0, 1, 3))
    return (station_adjoint, residual)


def solution(mesh):
    placed = (
        P("stn", "win", None, None),
        P("stn", None, None, None),
        P("stn"),
        P("stn"),
        P("stn", None, None),
        P("stn"),
        P("stn"),
    )
    return jax.shard_map(
        shards,
        mesh=mesh,
        in_specs=placed,
        out_specs=(P("stn", "win", None, None), P(("stn", "win"), None, None, None)),
        check_vma=False,
    )
```

```python
import functools
import math

import jax
import jax.numpy as jnp
from jax import lax
from jax.experimental import pallas as pl
from jax.experimental.pallas import tpu as pltpu
from jax.sharding import PartitionSpec as P

LAGS = 256
HALF = LAGS // 2
LANES = 128
HALF_TILE = LANES // 2
PHASES = 16
WIDE = 32
EARLY = 13
CHANS = 3
WINDOW = 3 * LANES
DEPTH = 7 * LANES


def member(me, chips, step, other):
    return 2 * ((me // 2 + step) & (chips - 1)) + ((me & 1) ^ other)


def near_slot(q, me, chips):
    return 2 * ((me // 2 - q // 2) & (chips - 1)) + ((q ^ me) & 1)


def fetch(sources, targets, sems):
    copies = [pltpu.make_async_copy(s, t, sems.at[k]) for k, (s, t) in enumerate(zip(sources, targets))]
    for copy in copies:
        copy.start()
    return copies


def pack_kernel(rows_in, rec_ref, swap_ref, *refs):
    keep_refs = refs[:-4]
    buffer, scratch, rows_ref, sems = refs[-4:]
    me = lax.axis_index("stn")
    stations = rec_ref.shape[1]
    chunks = rec_ref.shape[2] // LANES
    copies = fetch(
        [rows_in] + [rec_ref.at[c] for c in range(CHANS)],
        [rows_ref] + [buffer.at[c] for c in range(CHANS)],
        sems,
    )
    copies[0].wait()
    for c in range(CHANS):
        copies[c + 1].wait()
        for r in range(chunks):
            piece = buffer[c, :, r * LANES:(r + 1) * LANES]
            scratch[c, r * stations:(r + 1) * stations, :] = piece.astype(jnp.float32)
        for j, keep_ref in enumerate(keep_refs):
            for i, ref in enumerate((keep_ref, swap_ref.at[j])):
                station = rows_ref[member(me, len(keep_refs), j, i)]
                picked = scratch[c, pl.ds(station, chunks, stride=stations), :]
                ref[c] = picked.astype(jnp.bfloat16)


def unpack_kernel(order, rows_in, *refs):
    returned = refs[:-5]
    out_ref, buffer, scratch, rows_ref, sems = refs[-5:]
    rows_copy = pltpu.make_async_copy(rows_in, rows_ref, sems.at[CHANS])
    rows_copy.start()
    scratch[...] = jnp.zeros_like(scratch)
    rows_copy.wait()
    me = lax.axis_index("stn")
    stations = out_ref.shape[1]
    chunks = out_ref.shape[2] // LANES
    copies = []
    for c in range(CHANS):
        pieces = [(2 * j + i, ref.at[i]) for j, ref in zip(order, returned[:-2]) for i in range(2)]
        for j, ref in pieces + [(0, returned[-2]), (1, returned[-1])]:
            station = rows_ref[member(me, len(order) - 1, j // 2, j % 2)]
            where = pl.ds(station, chunks, stride=stations)
            scratch[c, where, :] = scratch[c, where, :] + ref[c].astype(jnp.float32)
        for r in range(chunks):
            piece = scratch[c, r * stations:(r + 1) * stations, :]
            buffer[c, :, r * LANES:(r + 1) * LANES] = piece.astype(jnp.bfloat16)
        copies.append(pltpu.make_async_copy(buffer.at[c], out_ref.at[c], sems.at[c]))
        copies[c].start()
    for copy in copies:
        copy.wait()


def build_phases(slot_refs, fan_ref, first_slot):
    chunks = slot_refs[0].shape[1]
    rows = fan_ref.shape[1]
    lane = lax.broadcasted_iota(jnp.int32, (LANES, LANES), 1)
    left = lax.broadcasted_iota(jnp.int32, (rows, LANES), 1) < chunks
    for place in range(0, CHANS * len(slot_refs), 2):
        pair = [slot_refs[e // CHANS][e % CHANS] for e in (place, place + 1)]
        middle = jnp.concatenate(pair, axis=0).astype(jnp.float32).T
        before = jnp.where(lane % chunks == 0, 0.0, pltpu.roll(middle, 1, 1))
        after = jnp.where(lane % chunks == chunks - 1, 0.0, pltpu.roll(middle, LANES - 1, 1))
        wide = jnp.concatenate([before, middle, after], axis=0)
        swapped = pltpu.roll(wide, chunks, 1)
        one = jnp.where(left, wide[:rows], swapped[HALF_TILE:])
        two = jnp.where(left, swapped[:rows], wide[HALF_TILE:])
        fan_ref[CHANS * first_slot + place] = one.astype(jnp.bfloat16)
        fan_ref[CHANS * first_slot + place + 1] = two.astype(jnp.bfloat16)


def shifted_rows(fan_ref, slot, phases):
    span = LAGS + phases
    tail = DEPTH - CHANS * span
    columns = []
    for first in range(0, HALF_TILE, phases):
        parts = [fan_ref[CHANS * slot + b, first:first + span, :] for b in range(CHANS)]
        parts.append(fan_ref[CHANS * slot, first:first + tail, :])
        columns.append(jnp.concatenate(parts, axis=0))
    return jnp.concatenate(columns, axis=1)


def prep_kernel(
    own_ref, got_ref, first_in, second_in, rows_in, low_in, high_in, observed_in,
    bands, fan_ref, first_out, second_out, rows_out, inside, seen, seen_later,
    staged, low_ref, high_ref, sems,
):
    copies = fetch(
        (low_in, high_in, observed_in, first_in, second_in, rows_in),
        (low_ref, high_ref, staged, first_out, second_out, rows_out),
        sems,
    )
    bands[...] = jnp.zeros_like(bands)
    build_phases([own_ref, got_ref], fan_ref, 0)
    for copy in copies:
        copy.wait()
    pairs = inside.shape[0]
    early = seen.shape[1]
    row = lax.broadcasted_iota(jnp.int32, (pairs, LAGS), 0)
    lag = lax.broadcasted_iota(jnp.int32, (pairs, LAGS), 1)
    low = jnp.zeros_like(row)
    high = jnp.zeros_like(row)
    for p in range(pairs):
        low = jnp.where(row == p, low_ref[p], low)
        high = jnp.where(row == p, high_ref[p], high)
    inside[...] = ((lag >= low) & (lag < high)).astype(jnp.int32)
    for i in range(seen.shape[0]):
        seen[i] = staged[i, :early]
        seen_later[i] = staged[i, early:]


def correlate(start, first_ref, second_ref, fan_ref, heads, corr_ref):
    me = lax.axis_index("stn")
    chips = heads.shape[0] // 2

    def step(p, carry):
        right = shifted_rows(fan_ref, near_slot(second_ref[start + p], me, chips), WIDE)
        products = lax.dot_general(
            heads[near_slot(first_ref[start + p], me, chips)], right, (((1,), (1,)), ((), ())),
            preferred_element_type=jnp.float32,
        )
        for a in range(CHANS):
            for b in range(CHANS):
                block = products[WIDE * a:WIDE * (a + 1), LAGS * b:LAGS * b + WINDOW]
                shift = WINDOW - WIDE * b - (WIDE - 1)
                turned = pltpu.roll(block, shift, 1, stride=1, stride_axis=0)
                corr_ref[CHANS * a + b, pl.ds(p, 1), :] = jnp.sum(
                    turned[:, :LAGS], axis=0, keepdims=True
                )
        return carry

    count = corr_ref.shape[1]
    lax.fori_loop(0, count, step, 0, unroll=min(count, 16))


def corr_first_kernel(order, first_in, second_in, fan_in, *refs):
    given = refs[:-6]
    corr_ref, fan_ref, heads, first_ref, second_ref, sems = refs[-6:]
    copies = fetch((first_in, second_in), (first_ref, second_ref), sems)
    slot_refs = [None] * (2 * len(given))
    for j, ref in zip(order, given):
        slot_refs[2 * j - 2:2 * j] = [ref.at[0], ref.at[1]]
    build_phases(slot_refs, fan_ref, 2)
    height = CHANS * WIDE
    row = lax.broadcasted_iota(jnp.int32, (height, height), 0)
    column = lax.broadcasted_iota(jnp.int32, (height, height), 1)
    same = row // WIDE == column // WIDE
    flip = (same & (row % WIDE + column % WIDE == WIDE - 1)).astype(jnp.bfloat16)

    def head(q, carry):
        rows = []
        for a in range(CHANS):
            pieces = []
            for m in range(0, HALF_TILE, WIDE):
                pieces.append(fan_ref[CHANS * q + a, HALF + m:HALF + m + WIDE, :])
            rows.append(jnp.concatenate(pieces, axis=1))
        natural = jnp.concatenate(rows, axis=0)
        heads[q] = jnp.dot(flip, natural, preferred_element_type=jnp.float32).astype(jnp.bfloat16)
        return carry

    lax.fori_loop(0, heads.shape[0], head, 0, unroll=8)
    for copy in copies:
        copy.wait()
    correlate(0, first_ref, second_ref, fan_ref, heads, corr_ref)


def corr_second_kernel(start, first_ref, second_ref, fan_ref, heads, corr_ref):
    correlate(start, first_ref, second_ref, fan_ref, heads, corr_ref)


def spread(lag_rows, combos, p):
    turned = []
    for c, combo in enumerate(combos):
        block = jnp.broadcast_to(lag_rows[combo, pl.ds(p, 1), :], (PHASES, WINDOW))
        turned.append(pltpu.roll(block, PHASES * c, 1, stride=1, stride_axis=0))
    w0, w1, w2 = turned
    return jnp.concatenate(
        [
            w0[:, :LAGS],
            w0[:, LAGS:] + w1[:, :LANES],
            w1[:, LANES:LAGS],
            w1[:, LAGS:] + w2[:, :LANES],
            w2[:, LANES:],
        ],
        axis=1,
    ).astype(jnp.bfloat16)


def pairwise(terms):
    while len(terms) > 1:
        terms = [sum(terms[k + 1:k + 2], terms[k]) for k in range(0, len(terms), 2)]
    return terms[0]


def residuals(corr_scale, part_refs, observed_ref, inside, resid, forward, backward):
    combos, pairs, _ = resid.shape
    flip = (
        lax.broadcasted_iota(jnp.int32, (LAGS, WINDOW), 0)
        + lax.broadcasted_iota(jnp.int32, (LAGS, WINDOW), 1)
        == LAGS
    ).astype(jnp.bfloat16)
    forward[:, :, LAGS:] = jnp.zeros((combos, pairs, WINDOW - LAGS), jnp.float32)
    for i in range(combos):
        summed = pairwise([ref[i] for ref in part_refs])
        value = jnp.where(inside, summed * corr_scale - observed_ref[i], 0.0)
        resid[i] = value
        rounded = value.astype(jnp.bfloat16)
        forward[i, :, :LAGS] = rounded.astype(jnp.float32)
        backward[i] = jnp.dot(rounded, flip, preferred_element_type=jnp.float32)


def fill_bands(start, first_ref, second_ref, forward, backward, bands):
    me = lax.axis_index("stn")
    slots = bands.shape[0]
    pairs = forward.shape[1]
    height = CHANS * PHASES

    def row_place(q):
        return q // 2 + (slots // 2) * (1 - q % 2)

    def fill(p, carry):
        qf = near_slot(first_ref[start + p], me, slots // 2)
        qs = near_slot(second_ref[start + p], me, slots // 2)
        for c in range(CHANS):
            at = pl.multiple_of(height * row_place(qf) + PHASES * c, PHASES)
            bands[qs, pl.ds(at, PHASES), :] = spread(
                forward, [CHANS * c + b for b in range(CHANS)], p
            )
            at = pl.multiple_of(height * row_place(qs) + PHASES * c, PHASES)
            bands[qf, pl.ds(at, PHASES), :] = spread(
                backward, [CHANS * a + c for a in range(CHANS)], p
            )
        return carry

    lax.fori_loop(0, pairs, fill, 0, unroll=min(pairs, 16))


def contract(adj_scale, first_row, bands, fan_ref, total, outs):
    rows = total.shape[0]
    slots = bands.shape[0]
    group = 2
    for r in range(0, slots, group):
        right = jnp.concatenate(
            [shifted_rows(fan_ref, q, PHASES) for q in range(r, r + group)], axis=0
        )
        left = jnp.concatenate(
            [bands[q, first_row:first_row + rows, :] for q in range(r, r + group)], axis=1
        )
        product = jnp.dot(left, right, preferred_element_type=jnp.float32)
        total[...] = product if r == 0 else total[...] + product
    chunks = outs[0].shape[1]
    near = lax.broadcasted_iota(jnp.int32, (PHASES, LANES), 1) < chunks
    for place in range(0, rows // PHASES, 2):
        upper = []
        lower = []
        for m in range(4):
            columns = slice(m * LANES, (m + 1) * LANES)
            one = total[place * PHASES:(place + 1) * PHASES, columns]
            two = total[(place + 1) * PHASES:(place + 2) * PHASES, columns]
            upper.append(jnp.where(near, one, pltpu.roll(two, chunks, 1)))
            lower.append(jnp.where(near, pltpu.roll(one, chunks, 1), two))
        tile = (jnp.concatenate(upper + lower, axis=0).T * adj_scale).astype(jnp.bfloat16)
        for k in range(2):
            e = place + k
            outs[e // CHANS][e % CHANS] = tile[k * chunks:(k + 1) * chunks]


def bands_kernel(corr_scale, first_in, second_in, inside_ref, seen_ref, bands_in, *refs):
    part_refs = refs[:-7]
    bands, resid, forward, backward, first_ref, second_ref, sems = refs[-7:]
    copies = fetch((first_in, second_in), (first_ref, second_ref), sems)
    inside = inside_ref[:resid.shape[1], :] > 0
    residuals(corr_scale, part_refs, seen_ref, inside, resid, forward, backward)
    for copy in copies:
        copy.wait()
    fill_bands(0, first_ref, second_ref, forward, backward, bands)


def adjoint_kernel(
    corr_scale, adj_scale, first_in, second_in, inside_ref, seen_ref, bands_in, fan_ref,
    earlier, *refs
):
    (bands, swap_ref, share_ref, resid, forward, backward, total,
     first_ref, second_ref, sems) = refs[-10:]
    part_refs = refs[:-10]
    copies = fetch((first_in, second_in), (first_ref, second_ref), sems)
    half = earlier.shape[1]
    inside = inside_ref[half:, :] > 0
    residuals(corr_scale, part_refs, seen_ref, inside, resid, forward, backward)
    offset = lax.axis_index("win") * share_ref.shape[1]
    for j in range(share_ref.shape[1]):
        p = offset + j
        for i in range(resid.shape[0]):
            one = earlier[i, pl.ds(jnp.minimum(p, half - 1), 1), :]
            two = resid[i, pl.ds(jnp.maximum(p - half, 0), 1), :]
            share_ref[i, j:j + 1, :] = jnp.where(p < half, one, two)
    for copy in copies:
        copy.wait()
    fill_bands(half, first_ref, second_ref, forward, backward, bands)
    outs = [swap_ref.at[j] for j in range(swap_ref.shape[0])]
    contract(adj_scale, 0, bands, fan_ref, total, outs)


def keep_kernel(adj_scale, bands, fan_ref, *refs):
    outs = refs[:-1]
    total = refs[-1]
    contract(adj_scale, total.shape[0], bands, fan_ref, total, outs)


def smem():
    return pl.BlockSpec(memory_space=pltpu.SMEM)


def vmem():
    return pl.BlockSpec(memory_space=pltpu.VMEM)


def flipped(x, axis, bits):
    count = lax.axis_size(axis)
    return lax.ppermute(x, axis, [(k, k ^ bits) for k in range(count)])


def across(swap, keep, sign, first):
    chips = len(keep)
    got = flipped(swap, "stn", 1)
    order = first(chips)
    blocks = []
    for j in order:
        pairs = [(k, (k + 2 * sign * j) % (2 * chips)) for k in range(2 * chips)]
        blocks.append(lax.ppermute(jnp.stack([keep[j], got[j]]), "stn", pairs))
    return order + [0, 0], blocks + [keep[0], got[0]]


def window_parts(corr):
    groups = lax.axis_size("win")
    if groups > 4:
        gathered = lax.all_gather(corr, "win")
        return [gathered[w] for w in range(groups)]
    return [corr] + [flipped(corr, "win", w) for w in range(1, groups)]


def shards(records, observed, lag_lo, lag_hi, send_table, pair_first, pair_second):
    owner_count = lax.axis_size("stn")
    window_groups = lax.axis_size("win")
    stations, local_windows, _, samples = records.shape
    send_rows = send_table.reshape(-1)
    slots = send_rows.shape[0]
    chunks = samples // LANES
    pairs = observed.shape[0]
    combos = CHANS * CHANS
    share = pairs // window_groups
    corr_scale = 1.0 / math.sqrt(samples * local_windows * window_groups)
    adj_scale = 1.0 / math.sqrt(CHANS * LAGS)

    chips = slots // 2
    block = jax.ShapeDtypeStruct((CHANS, chunks, LANES), jnp.bfloat16)
    blocks = jax.ShapeDtypeStruct((chips, CHANS, chunks, LANES), jnp.bfloat16)
    any_space = pl.BlockSpec(memory_space=pltpu.HBM)
    planes = jnp.transpose(records, (1, 2, 0, 3)).reshape(CHANS, stations, samples)
    planes = pltpu.with_memory_space_constraint(planes, pltpu.HBM)
    send_rows, pair_first, pair_second, lag_lo, lag_hi = [
        pltpu.with_memory_space_constraint(x, pltpu.HBM)
        for x in (send_rows, pair_first, pair_second, lag_lo, lag_hi)
    ]
    swap, *keep = pl.pallas_call(
        pack_kernel,
        in_specs=[any_space, any_space],
        out_specs=[vmem()] * (1 + chips),
        out_shape=[blocks] + [block] * chips,
        scratch_shapes=[
            pltpu.VMEM((CHANS, stations, samples), jnp.bfloat16),
            pltpu.VMEM((CHANS, chunks * stations, LANES), jnp.float32),
            pltpu.SMEM((slots,), jnp.int32),
            pltpu.SemaphoreType.DMA((CHANS + 1,)),
        ],
        compiler_params=pltpu.CompilerParams(vmem_limit_bytes=8 * 2**20),
        name="pack",
    )(send_rows, planes)
    rows = 3 * LANES - HALF_TILE
    early = pairs * EARLY // 16
    fan_shape = jax.ShapeDtypeStruct((slots * CHANS, rows, LANES), jnp.bfloat16)
    corr_shape = jax.ShapeDtypeStruct((combos, early, LAGS), jnp.float32)
    late_shape = jax.ShapeDtypeStruct((combos, pairs - early, LAGS), jnp.float32)
    index_shape = jax.ShapeDtypeStruct((pairs,), jnp.int32)
    height = slots * CHANS * PHASES
    bands_shape = jax.ShapeDtypeStruct((slots, height, DEPTH), jnp.bfloat16)
    index_scratch = pltpu.SMEM((pairs,), jnp.int32)
    small = pltpu.CompilerParams(vmem_limit_bytes=16 * 2**20)
    cost = pl.CostEstimate(flops=2 * 10**9, bytes_accessed=2**22, transcendentals=0)
    seen = jnp.transpose(observed, (1, 2, 0, 3)).reshape(combos, pairs, LAGS)
    seen = pltpu.with_memory_space_constraint(seen, pltpu.HBM)
    order, arrived = across(swap, keep, 1, lambda n: list(range(1,n)))
    bands, fan, firsts, seconds, rows_copy, inside, seen, seen_later = pl.pallas_call(
        prep_kernel,
        in_specs=[vmem()] * 2 + [any_space] * 6,
        out_specs=[vmem()] * 8,
        out_shape=[
            bands_shape,
            fan_shape,
            index_shape,
            index_shape,
            jax.ShapeDtypeStruct((slots,), jnp.int32),
            jax.ShapeDtypeStruct((pairs, LAGS), jnp.int32),
            corr_shape,
            late_shape,
        ],
        scratch_shapes=[
            pltpu.VMEM((combos, pairs, LAGS), jnp.float32),
            index_scratch,
            index_scratch,
            pltpu.SemaphoreType.DMA((6,)),
        ],
        compiler_params=small,
        cost_estimate=cost,
        name="prep",
    )(*arrived[-2:], pair_first, pair_second, send_rows, lag_lo, lag_hi, seen)

    corr, fan, heads = pl.pallas_call(
        functools.partial(corr_first_kernel, order),
        in_specs=[vmem()] * (chips + 2),
        out_specs=[vmem()] * 3,
        out_shape=[
            corr_shape,
            fan_shape,
            jax.ShapeDtypeStruct(
                (slots, CHANS * WIDE, HALF_TILE // WIDE * LANES), jnp.bfloat16
            ),
        ],
        scratch_shapes=[index_scratch, index_scratch, pltpu.SemaphoreType.DMA((2,))],
        input_output_aliases={2: 1},
        compiler_params=small,
        cost_estimate=cost,
        name="corr_first",
    )(firsts, seconds, fan, *arrived[:-2])
    parts = window_parts(corr)
    later = pl.pallas_call(
        functools.partial(corr_second_kernel, early),
        in_specs=[smem(), smem(), vmem(), vmem()],
        out_specs=vmem(),
        out_shape=late_shape,
        compiler_params=small,
        cost_estimate=cost,
        name="corr_second",
    )(firsts, seconds, fan, heads)
    later_parts = window_parts(later)

    lag_rows = pltpu.VMEM((combos, early, WINDOW), jnp.float32)
    bands, resid = pl.pallas_call(
        functools.partial(bands_kernel, corr_scale),
        in_specs=[vmem()] * (5 + len(parts)),
        out_specs=[vmem()] * 2,
        out_shape=[bands_shape, corr_shape],
        scratch_shapes=[
            lag_rows, lag_rows, index_scratch, index_scratch, pltpu.SemaphoreType.DMA((2,))
        ],
        input_output_aliases={4: 0},
        compiler_params=small,
        cost_estimate=cost,
        name="bands",
    )(firsts, seconds, inside, seen, bands, *parts)
    total = pltpu.VMEM((height // 2, 4 * LANES), jnp.float32)
    lag_rows = pltpu.VMEM((combos, pairs - early, WINDOW), jnp.float32)
    bands, swap, residual = pl.pallas_call(
        functools.partial(adjoint_kernel, corr_scale, adj_scale),
        in_specs=[vmem()] * (7 + len(later_parts)),
        out_specs=[vmem()] * 3,
        out_shape=[bands_shape, blocks, jax.ShapeDtypeStruct((combos, share, LAGS), jnp.float32)],
        scratch_shapes=[
            pltpu.VMEM((combos, pairs - early, LAGS), jnp.float32),
            lag_rows,
            lag_rows,
            total,
            index_scratch,
            index_scratch,
            pltpu.SemaphoreType.DMA((2,)),
        ],
        input_output_aliases={4: 0},
        compiler_params=small,
        cost_estimate=cost,
        name="adjoint",
    )(firsts, seconds, inside, seen_later, bands, fan, resid, *later_parts)
    keep = pl.pallas_call(
        functools.partial(keep_kernel, adj_scale),
        in_specs=[vmem()] * 2,
        out_specs=[vmem()] * chips,
        out_shape=[block] * chips,
        scratch_shapes=[total],
        compiler_params=small,
        cost_estimate=cost,
        name="keep",
    )(bands, fan)
    order, returned = across(swap, keep, -1, lambda n: list(range(n-1,0,-1)))
    stacked = pl.pallas_call(
        functools.partial(unpack_kernel, order),
        in_specs=[vmem()] * (chips + 2),
        out_specs=any_space,
        out_shape=jax.ShapeDtypeStruct((CHANS, stations, samples), jnp.bfloat16),
        scratch_shapes=[
            pltpu.VMEM((CHANS, stations, samples), jnp.bfloat16),
            pltpu.VMEM((CHANS, chunks * stations, LANES), jnp.float32),
            pltpu.SMEM((slots,), jnp.int32),
            pltpu.SemaphoreType.DMA((CHANS + 1,)),
        ],
        compiler_params=pltpu.CompilerParams(vmem_limit_bytes=8 * 2**20),
        name="unpack",
    )(rows_copy, *returned)
    station_adjoint = jnp.transpose(stacked.reshape(1, CHANS, stations, samples), (2, 0, 1, 3))
    residual = jnp.transpose(residual.reshape(CHANS, CHANS, share, LAGS), (2, 0, 1, 3))
    return (station_adjoint, residual)


def solution(mesh):
    placed = (
        P("stn", "win", None, None),
        P("stn", None, None, None),
        P("stn"),
        P("stn"),
        P("stn", None, None),
        P("stn"),
        P("stn"),
    )
    return jax.shard_map(
        shards,
        mesh=mesh,
        in_specs=placed,
        out_specs=(P("stn", "win", None, None), P(("stn", "win"), None, None, None)),
        check_vma=False,
    )
```
